256 devices in a mesh: dp: 32 (over x, z_lo, y), pipe: 8 (over z_hi, core).
Axes of the slice: x: 4, y: 4, z: 8 (z_hi: 4, z_lo: 2; z = z_hi * 2 + z_lo), core: 2. Of those that a mesh axis runs over, the one named last changes fastest.
Arguments:
- hidden_in: bfloat16 [32768, 2048], P(('dp', 'pipe')), may hold values from -24 to 24
- grad_out: bfloat16 [32768, 2048], P(('dp', 'pipe')), may hold values from -1.1953125 to 1.1953125
- w_query: bfloat16 [8, 2048, 512], P('pipe'), may hold values from -0.125 to 0.125
- w_key: bfloat16 [8, 2048, 512], P('pipe'), may hold values from -0.125 to 0.125
- w_value: bfloat16 [8, 2048, 512], P('pipe'), may hold values from -0.125 to 0.125
- w_out: bfloat16 [8, 512, 2048], P('pipe'), may hold values from -0.1875 to 0.1875
- pattern: int32 [4, 3], replicated, may hold values from 0 to 3, as said below
Outputs:
- hidden_out: bfloat16 [32768, 2048], P(('dp', 'pipe'))
- grad_in: bfloat16 [32768, 2048], P(('dp', 'pipe'))
- grad_query: float32 [8, 2048, 512], P('pipe', 'dp')
- grad_key: float32 [8, 2048, 512], P('pipe', 'dp')
- grad_value: float32 [8, 2048, 512], P('pipe', 'dp')
- grad_wout: float32 [8, 512, 2048], P('pipe', 'dp')
The draws below stay inside these ranges and needn't reach their ends.
Inputs may be any that keep to these rules, and one draw needn't show every extreme that they name: `pattern`: row i lists key blocks for query block i: entry 0 is i, entry 1 is the block before i (i itself for the first block), the others are blocks no later than i; a row may repeat an entry.
All inputs are finite; a program needn't handle non-finite values.
Results may differ from the reference program's by a relative error of at most 0.023.
Values may be sent and summed in bfloat16 or wider, within the bound.
A program may use at most 128 MiB of HBM per device.

```python
import math
import jax
import jax.numpy as jnp
from jax import lax

D = 2048
HEADS = 16
HDIM = 64
BLK = 32
KSEL = 3
SEQ = 128
HALF = 512
QB = 4
SLOTS = 8
REPLICAS = 32
ROWS = 32768


def draw_pattern(key, part):
    row_ids = jnp.arange(QB, dtype=jnp.int32)[:, None]
    raw_ints = jax.random.randint(key, (QB, KSEL), 0, 1048576, dtype=jnp.int32)
    picked = raw_ints % (row_ids + 1)
    slot_ids = jnp.arange(KSEL, dtype=jnp.int32)[None, :]
    previous = jnp.maximum(row_ids - 1, 0)
    return jnp.where(slot_ids == 0, row_ids, jnp.where(slot_ids == 1, previous, picked)).astype(jnp.int32)


def strengthened(values, own_key, source, target, parts, factor):
    def block_of(dim):
        return (jnp.arange(values.shape[dim]) // (values.shape[dim] // parts)).reshape((-1,) + (1,) * (values.ndim - 1 - dim))

    first = jax.random.permutation(own_key, parts)[block_of(target)]
    other_side = (block_of(target) + parts // 2) % parts
    return jnp.where((block_of(source) == first) | (block_of(source) == other_side), factor * values, values)


def shard_levels(own_key, shape, pieces, smallest, high):
    def one(axis_at, shards_of):
        draws = jax.random.uniform(jax.random.fold_in(jax.random.fold_in(own_key, 6), axis_at), (shards_of,), jnp.float32, smallest / len(pieces), high / len(pieces))
        return jnp.repeat(jnp.exp(draws), shape[axis_at] // shards_of).reshape((-1,) + (1,) * (len(shape) - axis_at - 1))

    loudness = one(*pieces[0])
    for cut in pieces[1:]:
        loudness = loudness * one(*cut)
    return loudness


def centred(rng, shape, deviation, bound, split=(), kind=jnp.bfloat16):
    entries = deviation * jax.random.normal(rng, shape, jnp.float32)
    if split:
        entries = entries * shard_levels(rng, shape, split, -0.22, 0.18)
    return jnp.clip(entries, -bound, bound).astype(kind)


def heavy_noise(key, extent, spread, reach, shards, heavy, kind=jnp.bfloat16):
    array = spread * jax.random.normal(key, extent, jnp.float32)
    if shards:
        array = array * shard_levels(key, extent, shards, -0.22, 0.18)
    return jnp.clip(strengthened(array, jax.random.fold_in(key, 3), *heavy), -reach, reach).astype(kind)


def setup_inputs(seed: int = 0) -> dict:
    seeds = jax.random.split(jax.random.key(seed), 8)
    hidden_in = heavy_noise(seeds[0], (ROWS, D), 1.0, 24.0, ((0, 256),), (0, 1, 256, 6.0))
    grad_out = centred(seeds[1], (ROWS, D), 0.2, 1.1953125, ((0, 256),))
    w_query = centred(seeds[2], (SLOTS, D, HALF), D ** -0.5, 0.125, ((0, 8),))
    w_key = centred(seeds[3], (SLOTS, D, HALF), D ** -0.5, 0.125, ((0, 8),))
    w_value = centred(seeds[4], (SLOTS, D, HALF), D ** -0.5, 0.125, ((0, 8),))
    w_out = centred(seeds[5], (SLOTS, HALF, D), (HEADS * HDIM) ** -0.5, 0.1875, ((0, 8),))
    pattern = draw_pattern(jax.random.fold_in(seeds[7], 71), 0)
    return dict(hidden_in=hidden_in, grad_out=grad_out, w_query=w_query, w_key=w_key, w_value=w_value, w_out=w_out, pattern=pattern)


NORM_EPS = 1e-05

def visible_mask(pattern, block_len):
    blocks, slot_count = pattern.shape
    equal_slot = pattern[:, :, None] == pattern[:, None, :]
    before = jnp.arange(slot_count)[None, :] < jnp.arange(slot_count)[:, None]
    repeated = jnp.any(equal_slot & before[None, :, :], axis=2)
    row_ids = jnp.arange(block_len)[:, None]
    column_ids = jnp.arange(block_len)[None, :]
    diagonal = pattern == jnp.arange(blocks, dtype=jnp.int32)[:, None]
    allowed = jnp.where(diagonal[:, :, None, None], (column_ids <= row_ids)[None, None], True)
    visible = allowed & jnp.logical_not(repeated)[:, :, None, None]
    return jnp.transpose(visible, (0, 2, 1, 3))

def contract(left_factor, right_factor):
    return lax.dot_general(left_factor, right_factor, (((0,), (0,)), ((), ())), preferred_element_type=jnp.float32)

def replica_sum(left_factor, right_factor):
    left_split = left_factor.reshape(2, REPLICAS, SEQ, left_factor.shape[1])
    right_split = right_factor.reshape(2, REPLICAS, SEQ, right_factor.shape[1])

    def add_replica(total, index):
        left_piece = lax.dynamic_index_in_dim(left_split, index, 1, keepdims=False).reshape(2 * SEQ, left_factor.shape[1])
        right_piece = lax.dynamic_index_in_dim(right_split, index, 1, keepdims=False).reshape(2 * SEQ, right_factor.shape[1])
        rounded = lax.optimization_barrier(contract(left_piece, right_piece).astype(jnp.bfloat16))
        return (total + rounded.astype(jnp.float32), None)
    start = jnp.zeros((left_factor.shape[1], right_factor.shape[1]), jnp.float32)
    total, unused = lax.scan(add_replica, start, jnp.arange(REPLICAS, dtype=jnp.int32))
    return total

def attend_forward(inputs, query_w, key_w, value_w, out_w, pattern, head_dim, block_len):
    amount, seq_len, features = inputs.shape
    blocks = seq_len // block_len
    head_count = query_w.shape[1] // head_dim
    input_f32 = inputs.astype(jnp.float32)
    factor = lax.rsqrt(lax.optimization_barrier(jnp.mean(input_f32 * input_f32, axis=-1, keepdims=True)) + NORM_EPS)
    normed = (input_f32 * factor).astype(jnp.bfloat16).reshape(amount * seq_len, features)
    query = jnp.dot(normed, query_w, preferred_element_type=jnp.float32).astype(jnp.bfloat16)
    key_proj = jnp.dot(normed, key_w, preferred_element_type=jnp.float32).astype(jnp.bfloat16)
    values = jnp.dot(normed, value_w, preferred_element_type=jnp.float32).astype(jnp.bfloat16)
    blocked = (amount, blocks, block_len, head_count, head_dim)
    query_blocks = query.reshape(blocked)
    keys_seen = jnp.take(key_proj.reshape(blocked), pattern, axis=1)
    values_seen = jnp.take(values.reshape(blocked), pattern, axis=1)
    inv_sqrt = 1.0 / math.sqrt(head_dim)
    scores = jnp.einsum('mqihd,mqsjhd->mqhisj', query_blocks.astype(jnp.float32), keys_seen.astype(jnp.float32)) * inv_sqrt
    visible = visible_mask(pattern, block_len)[None, :, None]
    expo = jnp.where(visible, jnp.exp(scores), 0.0)
    totals = lax.optimization_barrier(jnp.sum(expo, axis=(4, 5), keepdims=True))
    prob_f32 = expo / totals
    prob_bf16 = prob_f32.astype(jnp.bfloat16)
    attended = jnp.einsum('mqhisj,mqsjhd->mqihd', prob_bf16.astype(jnp.float32), values_seen.astype(jnp.float32))
    attended = attended.astype(jnp.bfloat16).reshape(amount * seq_len, head_count * head_dim)
    contrib = jnp.dot(attended, out_w, preferred_element_type=jnp.float32).astype(jnp.bfloat16)
    stash_fwd = (input_f32, factor, normed, query_blocks, keys_seen, values_seen, prob_f32, prob_bf16, attended)
    return (contrib.reshape(amount, seq_len, features), stash_fwd)

def attend_backward(stash_fwd, cotangent, query_w, key_w, value_w, out_w, pattern, head_dim, block_len):
    input_f32, factor, normed, query_blocks, keys_seen, values_seen, prob_f32, prob_bf16, attended = stash_fwd
    amount, seq_len, features = cotangent.shape
    blocks = seq_len // block_len
    head_count = query_w.shape[1] // head_dim
    inv_sqrt = 1.0 / math.sqrt(head_dim)
    grad_flat = cotangent.reshape(amount * seq_len, features)
    grad_attended = lax.dot_general(grad_flat, out_w, (((1,), (1,)), ((), ())), preferred_element_type=jnp.float32)
    grad_attended = grad_attended.astype(jnp.bfloat16).reshape(amount, blocks, block_len, head_count, head_dim)
    grad_prob = jnp.einsum('mqihd,mqsjhd->mqhisj', grad_attended.astype(jnp.float32), values_seen.astype(jnp.float32))
    grad_valseen = jnp.einsum('mqhisj,mqihd->mqsjhd', prob_bf16.astype(jnp.float32), grad_attended.astype(jnp.float32))
    inner_sum = lax.optimization_barrier(jnp.sum(prob_f32 * grad_prob, axis=(4, 5), keepdims=True))
    grad_score = (prob_f32 * (grad_prob - inner_sum) * inv_sqrt).astype(jnp.bfloat16)
    grad_querypos = jnp.einsum('mqhisj,mqsjhd->mqihd', grad_score.astype(jnp.float32), keys_seen.astype(jnp.float32))
    grad_querypos = grad_querypos.astype(jnp.bfloat16).reshape(amount * seq_len, head_count * head_dim)
    grad_keyseen = jnp.einsum('mqhisj,mqihd->mqsjhd', grad_score.astype(jnp.float32), query_blocks.astype(jnp.float32))
    onehot = (pattern[:, :, None] == jnp.arange(blocks, dtype=jnp.int32)[None, None, :]).astype(jnp.float32)
    grad_keypos = jnp.einsum('qsk,mqsjhd->mkjhd', onehot, grad_keyseen, precision=lax.Precision.HIGHEST)
    grad_keypos = grad_keypos.astype(jnp.bfloat16).reshape(amount * seq_len, head_count * head_dim)
    grad_valuepos = jnp.einsum('qsk,mqsjhd->mkjhd', onehot, grad_valseen, precision=lax.Precision.HIGHEST)
    grad_valuepos = grad_valuepos.astype(jnp.bfloat16).reshape(amount * seq_len, head_count * head_dim)
    dims = (((1,), (1,)), ((), ()))
    grad_normed = lax.dot_general(grad_querypos, query_w, dims, preferred_element_type=jnp.float32)
    grad_normed = grad_normed + lax.dot_general(grad_keypos, key_w, dims, preferred_element_type=jnp.float32)
    grad_normed = grad_normed + lax.dot_general(grad_valuepos, value_w, dims, preferred_element_type=jnp.float32)
    grad_normed = grad_normed.reshape(amount, seq_len, features)
    mean_term = lax.optimization_barrier(jnp.mean(input_f32 * grad_normed, axis=-1, keepdims=True))
    returned = (factor * grad_normed - input_f32 * factor * factor * factor * mean_term).astype(jnp.bfloat16)
    factor_pairs = ((normed, grad_querypos), (normed, grad_keypos), (normed, grad_valuepos), (attended, grad_flat))
    return (returned, factor_pairs)

def reference(hidden_in, grad_out, w_query, w_key, w_value, w_out, pattern):
    sequences = hidden_in.reshape(REPLICAS, SLOTS, SEQ, D)
    cotangents = grad_out.reshape(REPLICAS, SLOTS, SEQ, D)
    outputs = [None] * SLOTS
    input_grads = [None] * SLOTS
    grads = [[None] * SLOTS for position in range(4)]
    for section_idx in range(SLOTS // 2):
        slot_pair = (section_idx, SLOTS - 1 - section_idx)
        inputs = jnp.concatenate([sequences[:, slot_pair[0]], sequences[:, slot_pair[1]]], axis=0)
        cotangent = jnp.concatenate([cotangents[:, slot_pair[0]], cotangents[:, slot_pair[1]]], axis=0)
        summed_out = inputs.astype(jnp.float32)
        summed_in = cotangent.astype(jnp.float32)
        for slot_idx in slot_pair:
            contrib, stash_fwd = attend_forward(inputs, w_query[slot_idx], w_key[slot_idx], w_value[slot_idx], w_out[slot_idx], pattern, HDIM, BLK)
            returned, factor_pairs = attend_backward(stash_fwd, cotangent, w_query[slot_idx], w_key[slot_idx], w_value[slot_idx], w_out[slot_idx], pattern, HDIM, BLK)
            summed_out = summed_out + contrib.astype(jnp.float32)
            summed_in = summed_in + returned.astype(jnp.float32)
            for position in range(4):
                grads[position][slot_idx] = replica_sum(factor_pairs[position][0], factor_pairs[position][1])
        summed_out = summed_out.astype(jnp.bfloat16)
        summed_in = summed_in.astype(jnp.bfloat16)
        outputs[slot_pair[0]] = summed_out[:REPLICAS]
        outputs[slot_pair[1]] = summed_out[REPLICAS:]
        input_grads[slot_pair[0]] = summed_in[:REPLICAS]
        input_grads[slot_pair[1]] = summed_in[REPLICAS:]
    hidden_out = jnp.stack(outputs, axis=1).reshape(ROWS, D)
    grad_in = jnp.stack(input_grads, axis=1).reshape(ROWS, D)
    return (hidden_out, grad_in, jnp.stack(grads[0]), jnp.stack(grads[1]), jnp.stack(grads[2]), jnp.stack(grads[3]))
```

```python
import math

import jax
import jax.numpy as jnp
from jax import lax
from jax.experimental import pallas as pl
from jax.experimental.pallas import tpu as pltpu
from jax.sharding import PartitionSpec as P

HDIM = 64
BLK = 32


NORM_EPS = 1e-05


MESH = pl.DeviceIdType.MESH
X_SIZE, Z_SIZE, Y_SIZE = 4, 2, 4


def ring_scatter_kernel(*refs):
    count = 4
    parts = refs[:count]
    outs = refs[count : 2 * count]
    scratch = refs[2 * count :]
    far, near, far2, near2, last = (scratch[i * count : (i + 1) * count] for i in range(5))
    send_sem, recv_sem = scratch[5 * count], scratch[5 * count + 1]
    dp = lax.axis_index("dp")
    pipe = lax.axis_index("pipe")
    x_at = dp // (Z_SIZE * Y_SIZE)
    z_at = lax.rem(dp // Y_SIZE, Z_SIZE)
    y_at = lax.rem(dp, Y_SIZE)

    def device(x, z, y):
        return ((x * Z_SIZE + z) * Y_SIZE + y, pipe)

    def x_to(step):
        return device(lax.rem(x_at + step, X_SIZE), z_at, y_at)

    def y_to(step):
        return device(x_at, z_at, lax.rem(y_at + step, Y_SIZE))

    mate = device(x_at, 1 - z_at, y_at)
    barrier = pltpu.get_barrier_semaphore()
    for target in (x_to(1), x_to(3), y_to(1), y_to(3), mate):
        pl.semaphore_signal(barrier, inc=1, device_id=target, device_id_type=MESH)
    pl.semaphore_wait(barrier, 5)

    x_first = (True, True, False, False)
    order = (0, 2, 1, 3)
    started = []

    def copy(src, dst, t, slot, target):
        made = pltpu.make_async_remote_copy(
            src_ref=src,
            dst_ref=dst,
            send_sem=send_sem.at[t, slot],
            recv_sem=recv_sem.at[t, slot],
            device_id=target,
            device_id_type=MESH,
        )
        made.start()
        started.append(made)
        return made

    def total(*terms):
        acc = terms[0].astype(jnp.float32)
        for term in terms[1:]:
            acc = acc + term.astype(jnp.float32)
        return acc

    def ring(stage, base, take, here, send_to, far_bufs, near_bufs):
        msgs = {}
        for t in order:
            at = here[t]
            opposite = lax.rem(at + 2, 4)
            msgs[t, 0] = copy(take(t, opposite, 0), far_bufs[t].at[0], t, base, send_to(t, 1))
            msgs[t, 1] = copy(take(t, opposite, 1), far_bufs[t].at[1], t, base + 1, send_to(t, 3))
        for t in order:
            right, left = lax.rem(here[t] + 1, 4), lax.rem(here[t] + 3, 4)
            msgs[t, 2] = copy(take(t, right, 1), near_bufs[t].at[0, 1], t, base + 2, send_to(t, 1))
            msgs[t, 3] = copy(take(t, left, 0), near_bufs[t].at[1, 0], t, base + 3, send_to(t, 3))
        for t in order:
            right, left = lax.rem(here[t] + 1, 4), lax.rem(here[t] + 3, 4)
            msgs[t, 0].wait_recv()
            far_bufs[t][0] = total(take(t, right, 0)[...], far_bufs[t][0]).astype(jnp.bfloat16)
            msgs[t, 4] = copy(far_bufs[t].at[0], near_bufs[t].at[0, 0], t, base + 4, send_to(t, 1))
            msgs[t, 1].wait_recv()
            far_bufs[t][1] = total(take(t, left, 1)[...], far_bufs[t][1]).astype(jnp.bfloat16)
            msgs[t, 5] = copy(far_bufs[t].at[1], near_bufs[t].at[1, 1], t, base + 5, send_to(t, 3))
        return msgs

    def take_first(t, at, z):
        return parts[t].at[at, z] if x_first[t] else parts[t].at[:, z, at]

    def take_second(t, at, z):
        return near[t].at[0, z, at]

    first_at = [x_at if first else y_at for first in x_first]
    second_at = [y_at if first else x_at for first in x_first]
    msgs = ring(0, 0, take_first, first_at, lambda t, s: x_to(s) if x_first[t] else y_to(s), far, near)
    for t in order:
        for slot in range(2, 6):
            msgs[t, slot].wait_recv()
        for z in range(2):
            own = take_first(t, first_at[t], z)[...]
            near[t][0, z] = total(own, near[t][0, z], near[t][1, z]).astype(jnp.bfloat16)
    msgs = ring(1, 6, take_second, second_at, lambda t, s: y_to(s) if x_first[t] else x_to(s), far2, near2)
    finals = {}
    for t in order:
        for slot in range(2, 6):
            msgs[t, slot].wait_recv()
        for z in range(2):
            own = take_second(t, second_at[t], z)[...]
            near2[t][0, z] = total(own, near2[t][0, z], near2[t][1, z]).astype(jnp.bfloat16)
        finals[t] = copy(near2[t].at[0, 1 - z_at], last[t], t, 12, mate)
    for t in order:
        finals[t].wait_recv()
        outs[t][...] = total(near2[t][0, z_at], last[t][...])
    for made in started:
        made.wait_send()


def ring_scatter(parts):
    split = [p.reshape(X_SIZE, Z_SIZE, Y_SIZE, p.shape[0] // 32, p.shape[1]) for p in parts]
    tails = [p.shape[3:] for p in split]
    vmem = pl.BlockSpec(memory_space=pltpu.VMEM)
    bf16 = jnp.bfloat16
    return pl.pallas_call(
        ring_scatter_kernel,
        out_shape=tuple(jax.ShapeDtypeStruct(t, jnp.float32) for t in tails),
        in_specs=[vmem] * 4,
        out_specs=(vmem,) * 4,
        scratch_shapes=[pltpu.VMEM((2, 4) + t, bf16) for t in tails]
        + [pltpu.VMEM((2, 2, 4) + t, bf16) for t in tails]
        + [pltpu.VMEM((2,) + t, bf16) for t in tails]
        + [pltpu.VMEM((2, 2) + t, bf16) for t in tails]
        + [pltpu.VMEM(t, bf16) for t in tails]
        + [pltpu.SemaphoreType.DMA((4, 13)), pltpu.SemaphoreType.DMA((4, 13))],
        compiler_params=pltpu.CompilerParams(
            collective_id=0, has_side_effects=True, vmem_limit_bytes=40 * 1024 * 1024
        ),
        name="ring_scatter",
    )(*split)


def visible_mask(pattern, block_len):
    blocks, slot_count = pattern.shape
    equal_slot = pattern[:, :, None] == pattern[:, None, :]
    before = jnp.arange(slot_count)[None, :] < jnp.arange(slot_count)[:, None]
    repeated = jnp.any(equal_slot & before[None, :, :], axis=2)
    row_ids = jnp.arange(block_len)[:, None]
    column_ids = jnp.arange(block_len)[None, :]
    diagonal = pattern == jnp.arange(blocks, dtype=jnp.int32)[:, None]
    allowed = jnp.where(diagonal[:, :, None, None], (column_ids <= row_ids)[None, None], True)
    visible = allowed & jnp.logical_not(repeated)[:, :, None, None]
    return jnp.transpose(visible, (0, 2, 1, 3))


def contract(left_factor, right_factor):
    return lax.dot_general(
        left_factor, right_factor, (((0,), (0,)), ((), ())), preferred_element_type=jnp.float32
    )


def attend_forward(inputs, query_w, key_w, value_w, out_w, pattern, head_dim, block_len):
    amount, seq_len, features = inputs.shape
    blocks = seq_len // block_len
    head_count = query_w.shape[1] // head_dim
    input_f32 = inputs.astype(jnp.float32)
    factor = lax.rsqrt(jnp.mean(input_f32 * input_f32, axis=-1, keepdims=True) + NORM_EPS)
    normed = (input_f32 * factor).astype(jnp.bfloat16).reshape(amount * seq_len, features)
    query = jnp.dot(normed, query_w, preferred_element_type=jnp.float32).astype(jnp.bfloat16)
    key_proj = jnp.dot(normed, key_w, preferred_element_type=jnp.float32).astype(jnp.bfloat16)
    values = jnp.dot(normed, value_w, preferred_element_type=jnp.float32).astype(jnp.bfloat16)
    blocked = (amount, blocks, block_len, head_count, head_dim)
    query_blocks = query.reshape(blocked)
    keys_seen = jnp.take(key_proj.reshape(blocked), pattern, axis=1)
    values_seen = jnp.take(values.reshape(blocked), pattern, axis=1)
    inv_sqrt = 1.0 / math.sqrt(head_dim)
    scores = (
        jnp.einsum(
            "mqihd,mqsjhd->mqhisj", query_blocks, keys_seen, preferred_element_type=jnp.float32
        )
        * inv_sqrt
    )
    visible = visible_mask(pattern, block_len)[None, :, None]
    expo = jnp.where(visible, jnp.exp(scores), 0.0)
    totals = jnp.sum(expo, axis=(4, 5), keepdims=True)
    prob_f32 = expo / totals
    prob_bf16 = prob_f32.astype(jnp.bfloat16)
    attended = jnp.einsum(
        "mqhisj,mqsjhd->mqihd", prob_bf16, values_seen, preferred_element_type=jnp.float32
    )
    attended = attended.astype(jnp.bfloat16).reshape(amount * seq_len, head_count * head_dim)
    contrib = jnp.dot(attended, out_w, preferred_element_type=jnp.float32).astype(jnp.bfloat16)
    stash_fwd = (
        input_f32,
        factor,
        normed,
        query_blocks,
        keys_seen,
        values_seen,
        prob_f32,
        prob_bf16,
        attended,
    )
    return (contrib.reshape(amount, seq_len, features), stash_fwd)


def attend_backward(
    stash_fwd, cotangent, query_w, key_w, value_w, out_w, pattern, head_dim, block_len
):
    (
        input_f32,
        factor,
        normed,
        query_blocks,
        keys_seen,
        values_seen,
        prob_f32,
        prob_bf16,
        attended,
    ) = stash_fwd
    amount, seq_len, features = cotangent.shape
    blocks = seq_len // block_len
    head_count = query_w.shape[1] // head_dim
    inv_sqrt = 1.0 / math.sqrt(head_dim)
    grad_flat = cotangent.reshape(amount * seq_len, features)
    grad_attended = lax.dot_general(
        grad_flat, out_w, (((1,), (1,)), ((), ())), preferred_element_type=jnp.float32
    )
    grad_attended = grad_attended.astype(jnp.bfloat16).reshape(
        amount, blocks, block_len, head_count, head_dim
    )
    grad_prob = jnp.einsum(
        "mqihd,mqsjhd->mqhisj", grad_attended, values_seen, preferred_element_type=jnp.float32
    )
    grad_valseen = jnp.einsum(
        "mqhisj,mqihd->mqsjhd", prob_bf16, grad_attended, preferred_element_type=jnp.float32
    )
    inner_sum = jnp.sum(prob_f32 * grad_prob, axis=(4, 5), keepdims=True)
    grad_score = (prob_f32 * (grad_prob - inner_sum) * inv_sqrt).astype(jnp.bfloat16)
    grad_querypos = jnp.einsum(
        "mqhisj,mqsjhd->mqihd", grad_score, keys_seen, preferred_element_type=jnp.float32
    )
    grad_querypos = grad_querypos.astype(jnp.bfloat16).reshape(
        amount * seq_len, head_count * head_dim
    )
    grad_keyseen = jnp.einsum(
        "mqhisj,mqihd->mqsjhd", grad_score, query_blocks, preferred_element_type=jnp.float32
    )
    onehot = (pattern[:, :, None] == jnp.arange(blocks, dtype=jnp.int32)[None, None, :]).astype(
        jnp.float32
    )
    grad_keypos = jnp.einsum(
        "qsk,mqsjhd->mkjhd", onehot, grad_keyseen, precision=lax.Precision.HIGHEST
    )
    grad_keypos = grad_keypos.astype(jnp.bfloat16).reshape(amount * seq_len, head_count * head_dim)
    grad_valuepos = jnp.einsum(
        "qsk,mqsjhd->mkjhd", onehot, grad_valseen, precision=lax.Precision.HIGHEST
    )
    grad_valuepos = grad_valuepos.astype(jnp.bfloat16).reshape(
        amount * seq_len, head_count * head_dim
    )
    dims = (((1,), (1,)), ((), ()))
    grad_normed = lax.dot_general(grad_querypos, query_w, dims, preferred_element_type=jnp.float32)
    grad_normed = grad_normed + lax.dot_general(
        grad_keypos, key_w, dims, preferred_element_type=jnp.float32
    )
    grad_normed = grad_normed + lax.dot_general(
        grad_valuepos, value_w, dims, preferred_element_type=jnp.float32
    )
    grad_normed = grad_normed.reshape(amount, seq_len, features)
    mean_term = jnp.mean(input_f32 * grad_normed, axis=-1, keepdims=True)
    returned = (factor * grad_normed - input_f32 * factor * factor * factor * mean_term).astype(
        jnp.bfloat16
    )
    factor_pairs = (
        (normed, grad_querypos),
        (normed, grad_keypos),
        (normed, grad_valuepos),
        (attended, grad_flat),
    )
    return (returned, factor_pairs)


def on_device(hidden_in, grad_out, w_query, w_key, w_value, w_out, pattern):
    query_w = w_query[0]
    key_w = w_key[0]
    value_w = w_value[0]
    out_w = w_out[0]

    def mirror_single(payload):
        slots = lax.axis_size("pipe")
        return lax.ppermute(payload, "pipe", [(i, slots - 1 - i) for i in range(slots)])

    mirror_input = mirror_single(hidden_in)
    contrib, stash_fwd = attend_forward(
        jnp.stack([hidden_in, mirror_input]), query_w, key_w, value_w, out_w, pattern, HDIM, BLK
    )
    contrib_other = mirror_single(contrib[1])
    mirror_grad = mirror_single(grad_out)
    returned, factor_pairs = attend_backward(
        stash_fwd,
        jnp.stack([grad_out, mirror_grad]),
        query_w,
        key_w,
        value_w,
        out_w,
        pattern,
        HDIM,
        BLK,
    )
    returned_other = mirror_single(returned[1])
    hidden_out = (
        hidden_in.astype(jnp.float32)
        + contrib[0].astype(jnp.float32)
        + contrib_other.astype(jnp.float32)
    ).astype(jnp.bfloat16)
    grad_in = (
        grad_out.astype(jnp.float32)
        + returned[0].astype(jnp.float32)
        + returned_other.astype(jnp.float32)
    ).astype(jnp.bfloat16)
    full_grads = [contract(factor_pair[0], factor_pair[1]) for factor_pair in factor_pairs]
    shares = ring_scatter([full.astype(jnp.bfloat16) for full in full_grads])
    return (hidden_out, grad_in, shares[0][None], shares[1][None], shares[2][None], shares[3][None])


def solution(mesh):
    in_specs = (
        P(("dp", "pipe"), None),
        P(("dp", "pipe"), None),
        P("pipe", None, None),
        P("pipe", None, None),
        P("pipe", None, None),
        P("pipe", None, None),
        P(),
    )
    out_specs = (
        P(("dp", "pipe"), None),
        P(("dp", "pipe"), None),
        P("pipe", "dp", None),
        P("pipe", "dp", None),
        P("pipe", "dp", None),
        P("pipe", "dp", None),
    )
    return jax.shard_map(
        on_device, mesh=mesh, in_specs=in_specs, out_specs=out_specs, check_vma=False
    )
```

```python
import functools
import math

import jax
import jax.numpy as jnp
from jax import lax
from jax.experimental import pallas as pl
from jax.experimental.pallas import tpu as pltpu
from jax.sharding import PartitionSpec as P

HDIM = 64
BLK = 32
SEQ = 128
NORM_EPS = 1e-05
MESH = pl.DeviceIdType.MESH
X_SIZE, Z_SIZE, Y_SIZE = 4, 2, 4
RING_X = (False, True, False, True)
BF16 = jnp.bfloat16
F32 = jnp.float32


def dot_nn(a, b):
    return lax.dot_general(a, b, (((1,), (0,)), ((), ())), preferred_element_type=F32)


def dot_nt(a, b):
    return lax.dot_general(a, b, (((1,), (1,)), ((), ())), preferred_element_type=F32)


def dot_tn(a, b):
    return lax.dot_general(a, b, (((0,), (0,)), ((), ())), preferred_element_type=F32)


def total(*terms):
    acc = terms[0].astype(F32)
    for term in terms[1:]:
        acc = acc + term.astype(F32)
    return acc


def sublayer_kernel(*refs):
    pattern, x_in, g_in, wq_in, wk_in, wv_in, wo_in = refs[:7]
    hidden_out, grad_in, dwq_out, dwk_out, dwv_out, dwo_out = refs[7:13]
    (
        xs, gs, w_in, w_out, norm_t, att_t, qkv, prob, g_att, g_qkv, factor, g_norm,
        own_term, away_term, back_term, own_ret, away_ret, back_ret,
    ) = refs[13:31]
    parts, far, near, far2, near2, last = (refs[31 + 4 * i : 35 + 4 * i] for i in range(6))
    load_sem, pair_send, pair_recv, ring_send, ring_recv = refs[55:60]
    outs = (dwo_out, dwv_out, dwq_out, dwk_out)

    features = xs.shape[1]
    half = w_out.shape[0]
    heads = half // HDIM
    inv_sqrt = 1.0 / math.sqrt(HDIM)

    dp = lax.axis_index("dp")
    pipe = lax.axis_index("pipe")
    slots = lax.axis_size("pipe")
    x_at = dp // (Z_SIZE * Y_SIZE)
    z_at = lax.rem(dp // Y_SIZE, Z_SIZE)
    y_at = lax.rem(dp, Y_SIZE)

    def device(x, z, y):
        return ((x * Z_SIZE + z) * Y_SIZE + y, pipe)

    def x_to(step):
        return device(lax.rem(x_at + step, X_SIZE), z_at, y_at)

    def y_to(step):
        return device(x_at, z_at, lax.rem(y_at + step, Y_SIZE))

    z_mate = device(x_at, 1 - z_at, y_at)
    mirror = (dp, slots - 1 - pipe)

    first, second = pl.ds(0, SEQ), pl.ds(SEQ, SEQ)
    loads = [
        pltpu.make_async_copy(src, dst, load_sem.at[i])
        for i, (src, dst) in enumerate(
            (
                (x_in, xs.at[first]),
                (wq_in, w_in.at[:, pl.ds(0, half)]),
                (wk_in, w_in.at[:, pl.ds(half, half)]),
                (wv_in, w_in.at[:, pl.ds(2 * half, half)]),
                (wo_in, w_out),
                (g_in, gs.at[first]),
            )
        )
    ]
    for load in loads:
        load.start()

    barrier = pltpu.get_barrier_semaphore()
    for target in (mirror, x_to(1), x_to(3), y_to(1), y_to(3), z_mate):
        pl.semaphore_signal(barrier, inc=1, device_id=target, device_id_type=MESH)
    pl.semaphore_wait(barrier, 6)

    started = []

    def send(src, dst, send_sem, recv_sem, target):
        made = pltpu.make_async_remote_copy(
            src_ref=src, dst_ref=dst, send_sem=send_sem, recv_sem=recv_sem, device_id=target, device_id_type=MESH
        )
        made.start()
        started.append(made)
        return made

    def to_mirror(src, dst, slot):
        return send(src, dst, pair_send.at[slot], pair_recv.at[slot], mirror)

    x_move = to_mirror(x_in, xs.at[second], 0)
    g_move = to_mirror(g_in, gs.at[second], 1)

    row = lax.broadcasted_iota(jnp.int32, (SEQ, SEQ), 0)
    col = lax.broadcasted_iota(jnp.int32, (SEQ, SEQ), 1)
    row_block, col_block = row // BLK, col // BLK
    listed = None
    for j in range(pattern.shape[1]):
        entry = jnp.full((SEQ, SEQ), pattern[0, j], jnp.int32)
        for i in range(1, SEQ // BLK):
            entry = jnp.where(row_block == i, pattern[i, j], entry)
        hit = entry == col_block
        listed = hit if listed is None else jnp.logical_or(listed, hit)
    visible = jnp.logical_and(listed, jnp.logical_or(col_block != row_block, col <= row))
    mask = jnp.where(visible, 1.0, 0.0).astype(F32)

    def head(ref, rows, base, h):
        return ref[rows, base + h * HDIM : base + (h + 1) * HDIM]

    def forward(s):
        rows = slice(s * SEQ, (s + 1) * SEQ)

        def normalise(i, carry):
            at = pl.multiple_of(s * SEQ + i * 16, 16)
            chunk = xs[pl.ds(at, 16), :].astype(F32)
            scale = lax.rsqrt(jnp.mean(chunk * chunk, axis=-1, keepdims=True) + NORM_EPS)
            factor[pl.ds(at, 16), :] = jnp.broadcast_to(scale, (16, 128))
            own_norm[pl.ds(pl.multiple_of(i * 16, 16), 16), :] = (chunk * scale).astype(BF16)
            return carry

        own_norm = own_ret if s == 0 else away_ret
        lax.fori_loop(0, SEQ // 16, normalise, 0)
        for c in range(3):
            cols = slice(c * half, (c + 1) * half)
            qkv[rows, cols] = dot_nn(own_norm[...], w_in[:, cols]).astype(BF16)
        wide = min(512, features)
        for c in range(features // wide):
            norm_t[c * wide : (c + 1) * wide, rows] = own_norm[:, c * wide : (c + 1) * wide].T
        for h in range(0, heads, 2):
            pair = []
            for hh in (h, h + 1):
                score = dot_nt(head(qkv, rows, 0, hh), head(qkv, rows, half, hh)) * inv_sqrt
                expo = jnp.where(mask > 0.5, jnp.exp(score), 0.0)
                p = expo / jnp.sum(expo, axis=-1, keepdims=True)
                prob[s * heads + hh] = p
                pair.append(dot_nn(p.astype(BF16), head(qkv, rows, 2 * half, hh)).astype(BF16))
            both = jnp.concatenate(pair, axis=1)
            g_att[rows, h * HDIM : (h + 2) * HDIM] = both
        att_t[:, rows] = g_att[rows, :].T
        term = own_term if s == 0 else away_term
        for c in range(features // wide):
            cols = slice(c * wide, (c + 1) * wide)
            term[:, cols] = dot_nn(g_att[rows, :], w_out[:, cols]).astype(BF16)

    def backward_heads(s):
        rows = slice(s * SEQ, (s + 1) * SEQ)
        g_att[rows, :] = dot_nt(gs[rows, :], w_out[...]).astype(BF16)
        for h in range(0, heads, 2):
            g_q, g_k, g_v = [], [], []
            for hh in (h, h + 1):
                p = prob[s * heads + hh]
                ga = head(g_att, rows, 0, hh)
                g_prob = dot_nt(ga, head(qkv, rows, 2 * half, hh))
                inner = jnp.sum(p * g_prob, axis=-1, keepdims=True)
                g_score = (p * (g_prob - inner) * inv_sqrt).astype(BF16)
                g_q.append(dot_nn(g_score, head(qkv, rows, half, hh)).astype(BF16))
                g_k.append(dot_tn(g_score, head(qkv, rows, 0, hh)).astype(BF16))
                g_v.append(dot_tn(p.astype(BF16), ga).astype(BF16))
            for c, pieces in enumerate((g_q, g_k, g_v)):
                base = c * half + h * HDIM
                g_qkv[rows, base : base + 2 * HDIM] = jnp.concatenate(pieces, axis=1)

    def backward_input(s):
        rows = slice(s * SEQ, (s + 1) * SEQ)
        wide = min(512, features)
        for c in range(features // wide):
            cols = slice(c * wide, (c + 1) * wide)
            g_norm[:, cols] = dot_nt(g_qkv[rows, :], w_in[cols, :])
        result = own_ret if s == 0 else away_ret

        def returned(i, carry):
            at = pl.multiple_of(i * 16, 16)
            all_at = pl.multiple_of(s * SEQ + i * 16, 16)
            value = xs[pl.ds(all_at, 16), :].astype(F32)
            grad = g_norm[pl.ds(at, 16), :]
            r = factor[pl.ds(all_at, 16), 0:1]
            mean_term = jnp.mean(value * grad, axis=-1, keepdims=True)
            result[pl.ds(at, 16), :] = (r * grad - value * (r * r * r * mean_term)).astype(BF16)
            return carry

        lax.fori_loop(0, SEQ // 16, returned, 0)

    def copy(src, dst, t, slot, target):
        return send(src, dst, ring_send.at[t, slot], ring_recv.at[t, slot], target)

    def part_piece(t, at, z):
        return parts[t].at[at, z] if RING_X[t] else parts[t].at[:, z, at]

    def sum_piece(t, at, z):
        return near[t].at[0, z, at]

    def ring_to(t, stage, step):
        return x_to(step) if RING_X[t] == (stage == 0) else y_to(step)

    def ring_at(t, stage):
        return x_at if RING_X[t] == (stage == 0) else y_at

    msgs = {}

    def ring_start(t, stage):
        piece = (part_piece, sum_piece)[stage]
        far_buf, near_buf = ((far, near), (far2, near2))[stage]
        at, base = ring_at(t, stage), 6 * stage
        opposite, right, left = (lax.rem(at + step, 4) for step in (2, 1, 3))
        msgs[t, base] = copy(piece(t, opposite, 0), far_buf[t].at[0], t, base, ring_to(t, stage, 1))
        msgs[t, base + 1] = copy(piece(t, opposite, 1), far_buf[t].at[1], t, base + 1, ring_to(t, stage, 3))
        msgs[t, base + 2] = copy(piece(t, right, 1), near_buf[t].at[0, 1], t, base + 2, ring_to(t, stage, 1))
        msgs[t, base + 3] = copy(piece(t, left, 0), near_buf[t].at[1, 0], t, base + 3, ring_to(t, stage, 3))

    def ring_forward(t, stage):
        piece = (part_piece, sum_piece)[stage]
        far_buf, near_buf = ((far, near), (far2, near2))[stage]
        at, base = ring_at(t, stage), 6 * stage
        for side, step in ((0, 1), (1, 3)):
            msgs[t, base + side].wait_recv()
            own = piece(t, lax.rem(at + step, 4), side)[...]
            far_buf[t][side] = total(own, far_buf[t][side]).astype(BF16)
            msgs[t, base + 4 + side] = copy(
                far_buf[t].at[side], near_buf[t].at[side, side], t, base + 4 + side, ring_to(t, stage, step)
            )

    def ring_finish(t, stage):
        piece = (part_piece, sum_piece)[stage]
        near_buf = (near, near2)[stage]
        at, base = ring_at(t, stage), 6 * stage
        for slot in range(2, 6):
            msgs[t, base + slot].wait_recv()
        for z in range(2):
            own = piece(t, at, z)[...]
            near_buf[t][0, z] = total(own, near_buf[t][0, z], near_buf[t][1, z]).astype(BF16)

    def weight_grad(t, lhs, rhs):
        block = lhs.shape[0] // X_SIZE
        for i in range(X_SIZE):
            value = dot_nn(lhs[i * block : (i + 1) * block, :], rhs()).astype(BF16)
            parts[t][i] = value.reshape(parts[t].shape[1:])

    def grad_cols(c):
        return lambda: g_qkv[:, c * half : (c + 1) * half]

    for load in loads[:4]:
        load.wait()
    forward_ready = loads[4]
    forward_ready.wait()
    forward(0)
    loads[5].wait()
    backward_heads(0)
    backward_input(0)

    x_move.wait_recv()
    forward(1)
    term_move = to_mirror(away_term, back_term, 2)
    g_move.wait_recv()
    weight_grad(0, att_t, lambda: gs[...])
    ring_start(0, 0)
    backward_heads(1)
    weight_grad(1, norm_t, grad_cols(2))
    ring_start(1, 0)
    weight_grad(2, norm_t, grad_cols(0))
    ring_start(2, 0)
    weight_grad(3, norm_t, grad_cols(1))
    ring_start(3, 0)
    ring_forward(0, 0)
    backward_input(1)
    ret_move = to_mirror(away_ret, back_ret, 3)
    for t in (1, 2, 3):
        ring_forward(t, 0)
    for t in range(4):
        ring_finish(t, 0)
        ring_start(t, 1)
    for t in range(4):
        ring_forward(t, 1)

    def add_up(out, base, one, two):
        def body(i, carry):
            at = pl.ds(pl.multiple_of(i * 16, 16), 16)
            out[at, :] = total(base[at, :], one[at, :], two[at, :]).astype(BF16)
            return carry

        lax.fori_loop(0, SEQ // 16, body, 0)

    term_move.wait_recv()
    add_up(hidden_out, xs, own_term, back_term)
    finals = []
    for t in range(4):
        ring_finish(t, 1)
        finals.append(copy(near2[t].at[0, 1 - z_at], last[t], t, 12, z_mate))
    ret_move.wait_recv()
    add_up(grad_in, gs, own_ret, back_ret)
    for t in range(4):
        finals[t].wait_recv()
        outs[t][...] = total(near2[t][0, z_at], last[t][...])
    for made in started:
        made.wait_send()


def on_device(hidden_in, grad_out, w_query, w_key, w_value, w_out, pattern):
    features, half = w_query.shape[1], w_query.shape[2]
    heads = half // HDIM
    vmem = pl.BlockSpec(memory_space=pltpu.VMEM)
    anywhere = pl.BlockSpec(memory_space=pl.ANY)
    ranks = X_SIZE * Z_SIZE * Y_SIZE
    tails = [(half // ranks, features)] + [(features // ranks, half)] * 3
    both, one = (2 * SEQ, features), (SEQ, features)
    scratch = [
        pltpu.VMEM(both, BF16),
        pltpu.VMEM(both, BF16),
        pltpu.VMEM((features, 3 * half), BF16),
        pltpu.VMEM((half, features), BF16),
        pltpu.VMEM((features, 2 * SEQ), BF16),
        pltpu.VMEM((half, 2 * SEQ), BF16),
        pltpu.VMEM((2 * SEQ, 3 * half), BF16),
        pltpu.VMEM((2 * heads, SEQ, SEQ), F32),
        pltpu.VMEM((2 * SEQ, half), BF16),
        pltpu.VMEM((2 * SEQ, 3 * half), BF16),
        pltpu.VMEM((2 * SEQ, 128), F32),
        pltpu.VMEM(one, F32),
    ] + [pltpu.VMEM(one, BF16)] * 6
    for lead in ((X_SIZE, Z_SIZE, Y_SIZE), (2, 4), (2, 2, 4), (2,), (2, 2), ()):
        scratch += [pltpu.VMEM(lead + tail, BF16) for tail in tails]
    scratch += [
        pltpu.SemaphoreType.DMA((6,)),
        pltpu.SemaphoreType.DMA((4,)),
        pltpu.SemaphoreType.DMA((4,)),
        pltpu.SemaphoreType.DMA((4, 13)),
        pltpu.SemaphoreType.DMA((4, 13)),
    ]
    outs = pl.pallas_call(
        sublayer_kernel,
        out_shape=(jax.ShapeDtypeStruct(one, BF16),) * 2
        + tuple(jax.ShapeDtypeStruct(tail, F32) for tail in tails[1:] + tails[:1]),
        in_specs=[pl.BlockSpec(memory_space=pltpu.SMEM)] + [anywhere] * 6,
        out_specs=(vmem,) * 6,
        scratch_shapes=scratch,
        compiler_params=pltpu.CompilerParams(
            collective_id=0, has_side_effects=True, vmem_limit_bytes=56 * 1024 * 1024
        ),
        name="sublayer",
    )(pattern, hidden_in, grad_out, w_query[0], w_key[0], w_value[0], w_out[0])
    return (outs[0], outs[1]) + tuple(out[None] for out in outs[2:])


def solution(mesh):
    in_specs = (
        P(("dp", "pipe"), None),
        P(("dp", "pipe"), None),
        P("pipe", None, None),
        P("pipe", None, None),
        P("pipe", None, None),
        P("pipe", None, None),
        P(),
    )
    out_specs = (
        P(("dp", "pipe"), None),
        P(("dp", "pipe"), None),
        P("pipe", "dp", None),
        P("pipe", "dp", None),
        P("pipe", "dp", None),
        P("pipe", "dp", None),
    )
    return jax.shard_map(
        on_device, mesh=mesh, in_specs=in_specs, out_specs=out_specs, check_vma=False
    )
```

```python
import functools
import math

import jax
import jax.numpy as jnp
from jax import lax
from jax.experimental import pallas as pl
from jax.experimental.pallas import tpu as pltpu
from jax.sharding import PartitionSpec as P

HDIM = 64
BLK = 32
SEQ = 128
NORM_EPS = 1e-05
MESH = pl.DeviceIdType.MESH
X_SIZE, Z_SIZE, Y_SIZE = 4, 2, 4
RING_X = (False, True, True, True)
STEPS = (1, 3, 2)
BF16 = jnp.bfloat16
F32 = jnp.float32


def dot_nn(a, b):
    return lax.dot_general(a, b, (((1,), (0,)), ((), ())), preferred_element_type=F32)


def dot_nt(a, b):
    return lax.dot_general(a, b, (((1,), (1,)), ((), ())), preferred_element_type=F32)


def dot_tn(a, b):
    return lax.dot_general(a, b, (((0,), (0,)), ((), ())), preferred_element_type=F32)


def total(*terms):
    acc = terms[0].astype(F32)
    for term in terms[1:]:
        acc = acc + term.astype(F32)
    return acc


def sublayer_kernel(*refs):
    pattern, x_in, g_in, wq_in, wk_in, wv_in, wo_in = refs[:7]
    hidden_out, grad_in, dwq_out, dwk_out, dwv_out, dwo_out = refs[7:13]
    (
        xs, gs, w_in, w_out, norm_t, att_t, qkv, prob, g_att, g_qkv, factor, g_norm,
        own_term, away_term, back_term, own_ret, away_ret, back_ret,
        norm_y, grad_y, att_x, g_x, out_sum, out_recv,
    ) = refs[13:37]
    parts, far, near, last = (refs[37 + 4 * i : 41 + 4 * i] for i in range(4))
    load_sem, pair_send, pair_recv, ring_send, ring_recv, gather_send, gather_recv = refs[53:60]
    outs = (dwo_out, dwv_out, dwq_out, dwk_out)

    features = xs.shape[1]
    half = w_out.shape[0]
    heads = half // HDIM
    inv_sqrt = 1.0 / math.sqrt(HDIM)
    quarter = features // 4

    dp = lax.axis_index("dp")
    pipe = lax.axis_index("pipe")
    slots = lax.axis_size("pipe")
    x_at = dp // (Z_SIZE * Y_SIZE)
    z_at = lax.rem(dp // Y_SIZE, Z_SIZE)
    y_at = lax.rem(dp, Y_SIZE)

    def device(x, z, y):
        return ((x * Z_SIZE + z) * Y_SIZE + y, pipe)

    def x_to(step):
        return device(lax.rem(x_at + step, X_SIZE), z_at, y_at)

    def y_to(step):
        return device(x_at, z_at, lax.rem(y_at + step, Y_SIZE))

    z_mate = device(x_at, 1 - z_at, y_at)
    mirror = (dp, slots - 1 - pipe)

    first, second = pl.ds(0, SEQ), pl.ds(SEQ, SEQ)
    loads = [
        pltpu.make_async_copy(src, dst, load_sem.at[i])
        for i, (src, dst) in enumerate(
            (
                (x_in, xs.at[first]),
                (wq_in, w_in.at[:, pl.ds(0, half)]),
                (wk_in, w_in.at[:, pl.ds(half, half)]),
                (wv_in, w_in.at[:, pl.ds(2 * half, half)]),
                (wo_in, w_out),
                (g_in, gs.at[first]),
            )
        )
    ]
    for load in loads:
        load.start()

    barrier = pltpu.get_barrier_semaphore()
    for target in (mirror, z_mate) + tuple(to(step) for to in (x_to, y_to) for step in STEPS):
        pl.semaphore_signal(barrier, inc=1, device_id=target, device_id_type=MESH)
    pl.semaphore_wait(barrier, 8)

    started = []

    def send(src, dst, send_sem, recv_sem, target):
        made = pltpu.make_async_remote_copy(
            src_ref=src, dst_ref=dst, send_sem=send_sem, recv_sem=recv_sem, device_id=target, device_id_type=MESH
        )
        made.start()
        started.append(made)
        return made

    def to_mirror(src, dst, slot):
        return send(src, dst, pair_send.at[slot], pair_recv.at[slot], mirror)

    x_move = to_mirror(x_in, xs.at[second], 0)
    g_move = to_mirror(g_in, gs.at[second], 1)

    gathers = {}

    def gather(kind, src_of, dst_of, to):
        gathers[kind] = [
            send(src_of(step), dst_of(3 - step), gather_send.at[kind, i], gather_recv.at[kind, i], to(step))
            for i, step in enumerate(STEPS)
        ]

    def arrived(*kinds):
        for kind in kinds:
            for move in gathers[kind]:
                move.wait_recv()

    def seq(s):
        return pl.ds(s * SEQ, SEQ)

    def gather_norm(s):
        gather(
            s,
            lambda step: norm_t.at[:, lax.rem(y_at + step, 4), :, seq(s)],
            lambda i: norm_y.at[i, :, :, seq(s)],
            y_to,
        )

    def gather_att(s):
        gather(2 + s, lambda step: att_t.at[:, seq(s)], lambda i: att_x.at[i, :, seq(s)], x_to)

    def gather_out_grad(s):
        def piece(step):
            column = pl.multiple_of(lax.rem(x_at + step, 4) * quarter, quarter)
            return gs.at[seq(s), pl.ds(column, quarter)]

        gather(4 + s, piece, lambda i: g_x.at[i, seq(s), :], x_to)

    def gather_grad(s, c):
        cols = pl.ds(c * half, half)
        gather(6 + 3 * s + c, lambda step: g_qkv.at[seq(s), cols], lambda i: grad_y.at[i, seq(s), cols], y_to)

    row = lax.broadcasted_iota(jnp.int32, (SEQ, SEQ), 0)
    col = lax.broadcasted_iota(jnp.int32, (SEQ, SEQ), 1)
    row_block, col_block = row // BLK, col // BLK
    listed = None
    for j in range(pattern.shape[1]):
        entry = jnp.full((SEQ, SEQ), pattern[0, j], jnp.int32)
        for i in range(1, SEQ // BLK):
            entry = jnp.where(row_block == i, pattern[i, j], entry)
        hit = entry == col_block
        listed = hit if listed is None else jnp.logical_or(listed, hit)
    visible = jnp.logical_and(listed, jnp.logical_or(col_block != row_block, col <= row))
    mask = jnp.where(visible, 1.0, 0.0).astype(F32)

    def head(ref, rows, base, h):
        return ref[rows, base + h * HDIM : base + (h + 1) * HDIM]

    def forward(s):
        rows = slice(s * SEQ, (s + 1) * SEQ)

        def normalise(i, carry):
            at = pl.multiple_of(s * SEQ + i * 16, 16)
            chunk = xs[pl.ds(at, 16), :].astype(F32)
            scale = lax.rsqrt(jnp.mean(chunk * chunk, axis=-1, keepdims=True) + NORM_EPS)
            factor[pl.ds(at, 16), :] = jnp.broadcast_to(scale, (16, 128))
            own_norm[pl.ds(pl.multiple_of(i * 16, 16), 16), :] = (chunk * scale).astype(BF16)
            return carry

        own_norm = own_ret if s == 0 else away_ret
        lax.fori_loop(0, SEQ // 16, normalise, 0)
        for c in range(4):
            flipped = own_norm[:, c * quarter : (c + 1) * quarter].T
            norm_t[2 * c : 2 * c + 2, :, :, rows] = flipped.reshape((2,) + norm_t.shape[1:3] + (SEQ,))
        gather_norm(s)
        for c in range(3):
            cols = slice(c * half, (c + 1) * half)
            qkv[rows, cols] = dot_nn(own_norm[...], w_in[:, cols]).astype(BF16)
        wide = min(512, features)
        for h in range(0, heads, 2):
            pair = []
            for hh in (h, h + 1):
                score = dot_nt(head(qkv, rows, 0, hh), head(qkv, rows, half, hh)) * inv_sqrt
                expo = jnp.where(mask > 0.5, jnp.exp(score), 0.0)
                p = expo / jnp.sum(expo, axis=-1, keepdims=True)
                prob[s * heads + hh] = p
                pair.append(dot_nn(p.astype(BF16), head(qkv, rows, 2 * half, hh)).astype(BF16))
            both = jnp.concatenate(pair, axis=1)
            g_att[rows, h * HDIM : (h + 2) * HDIM] = both
        att_t[:, rows] = g_att[rows, :].T
        gather_att(s)
        term = own_term if s == 0 else away_term
        for c in range(features // wide):
            cols = slice(c * wide, (c + 1) * wide)
            term[:, cols] = dot_nn(g_att[rows, :], w_out[:, cols]).astype(BF16)

    def backward_heads(s):
        rows = slice(s * SEQ, (s + 1) * SEQ)
        g_att[rows, :] = dot_nt(gs[rows, :], w_out[...]).astype(BF16)
        for h in range(0, heads, 2):
            g_q, g_k, g_v = [], [], []
            for hh in (h, h + 1):
                p = prob[s * heads + hh]
                ga = head(g_att, rows, 0, hh)
                g_prob = dot_nt(ga, head(qkv, rows, 2 * half, hh))
                inner = jnp.sum(p * g_prob, axis=-1, keepdims=True)
                g_score = (p * (g_prob - inner) * inv_sqrt).astype(BF16)
                g_q.append(dot_nn(g_score, head(qkv, rows, half, hh)).astype(BF16))
                g_k.append(dot_tn(g_score, head(qkv, rows, 0, hh)).astype(BF16))
                g_v.append(dot_tn(p.astype(BF16), ga).astype(BF16))
            for c, pieces in enumerate((g_q, g_k, g_v)):
                base = c * half + h * HDIM
                g_qkv[rows, base : base + 2 * HDIM] = jnp.concatenate(pieces, axis=1)
        for c in (2, 0, 1):
            gather_grad(s, c)

    def backward_input(s):
        rows = slice(s * SEQ, (s + 1) * SEQ)
        wide = min(512, features)
        for c in range(features // wide):
            cols = slice(c * wide, (c + 1) * wide)
            g_norm[:, cols] = dot_nt(g_qkv[rows, :], w_in[cols, :])
        result = own_ret if s == 0 else away_ret

        def returned(i, carry):
            at = pl.multiple_of(i * 16, 16)
            all_at = pl.multiple_of(s * SEQ + i * 16, 16)
            value = xs[pl.ds(all_at, 16), :].astype(F32)
            grad = g_norm[pl.ds(at, 16), :]
            r = factor[pl.ds(all_at, 16), 0:1]
            mean_term = jnp.mean(value * grad, axis=-1, keepdims=True)
            result[pl.ds(at, 16), :] = (r * grad - value * (r * r * r * mean_term)).astype(BF16)
            return carry

        lax.fori_loop(0, SEQ // 16, returned, 0)

    msgs = {}

    def piece(t, at, z):
        return parts[t].at[at, z] if RING_X[t] else parts[t].at[:, z, at]

    def ring_to(t, step):
        return x_to(step) if RING_X[t] else y_to(step)

    def copy(src, dst, t, slot, target):
        msgs[t, slot] = send(src, dst, ring_send.at[t, slot], ring_recv.at[t, slot], target)

    def ring_start(t):
        at = x_at if RING_X[t] else y_at
        opposite, right, left = (lax.rem(at + step, 4) for step in (2, 1, 3))
        copy(piece(t, opposite, 0), far[t].at[0], t, 0, ring_to(t, 1))
        copy(piece(t, opposite, 1), far[t].at[1], t, 1, ring_to(t, 3))
        copy(piece(t, right, 1), near[t].at[0, 1], t, 2, ring_to(t, 1))
        copy(piece(t, left, 0), near[t].at[1, 0], t, 3, ring_to(t, 3))

    def ring_forward(t):
        at = x_at if RING_X[t] else y_at
        for side, step in ((0, 1), (1, 3)):
            msgs[t, side].wait_recv()
            own = piece(t, lax.rem(at + step, 4), side)[...]
            far[t][side] = total(own, far[t][side]).astype(BF16)
            copy(far[t].at[side], near[t].at[side, side], t, 4 + side, ring_to(t, step))

    def ring_finish(t):
        at = x_at if RING_X[t] else y_at
        for slot in range(2, 6):
            msgs[t, slot].wait_recv()
        for z in range(2):
            own = piece(t, at, z)[...]
            near[t][0, z] = total(own, near[t][0, z], near[t][1, z]).astype(BF16)
        copy(near[t].at[0, 1 - z_at], last[t], t, 6, z_mate)

    def weight_grad(t, c):
        cols = slice(c * half, (c + 1) * half)
        for i in range(X_SIZE):
            tall = (quarter // 4, 2 * SEQ)
            acc = dot_nn(norm_t[2 * i : 2 * i + 2, y_at].reshape(tall), g_qkv[:, cols])
            for j in range(3):
                acc = acc + dot_nn(norm_y[j, 2 * i : 2 * i + 2].reshape(tall), grad_y[j, :, cols])
            parts[t][i] = acc.astype(BF16).reshape(parts[t].shape[1:])

    def out_weight_grad():
        block = half // X_SIZE
        mine = gs[:, pl.ds(pl.multiple_of(x_at * quarter, quarter), quarter)]
        for i in range(X_SIZE):
            rows = slice(i * block, (i + 1) * block)
            acc = dot_nn(att_t[rows, :], mine)
            for j in range(3):
                acc = acc + dot_nn(att_x[j, rows, :], g_x[j])
            parts[0][i] = acc.astype(BF16).reshape(parts[0].shape[1:])

    for load in loads:
        load.wait()
    gather_out_grad(0)
    forward(0)
    backward_heads(0)
    backward_input(0)

    x_move.wait_recv()
    forward(1)
    term_move = to_mirror(away_term, back_term, 2)
    g_move.wait_recv()
    gather_out_grad(1)
    backward_heads(1)
    backward_input(1)
    ret_move = to_mirror(away_ret, back_ret, 3)
    arrived(2, 3, 4, 5)
    out_weight_grad()
    ring_start(0)
    arrived(0, 1, 8, 11)
    weight_grad(1, 2)
    ring_start(1)
    ring_forward(0)
    arrived(6, 9)
    weight_grad(2, 0)
    ring_start(2)
    ring_forward(1)
    arrived(7, 10)
    weight_grad(3, 1)
    ring_start(3)
    ring_finish(0)
    ring_forward(2)
    ring_finish(1)
    ring_forward(3)
    msgs[0, 6].wait_recv()
    out_sum[...] = total(near[0][0, z_at], last[0][...])
    spread = [
        send(out_sum.at[lax.rem(x_at + step, 4)], out_recv.at[3 - step], ring_send.at[0, 7 + i], ring_recv.at[0, 7 + i], x_to(step))
        for i, step in enumerate(STEPS)
    ]

    def add_up(out, base, one, two):
        def body(i, carry):
            at = pl.ds(pl.multiple_of(i * 16, 16), 16)
            out[at, :] = total(base[at, :], one[at, :], two[at, :]).astype(BF16)
            return carry

        lax.fori_loop(0, SEQ // 16, body, 0)

    term_move.wait_recv()
    add_up(hidden_out, xs, own_term, back_term)
    ring_finish(2)
    ring_finish(3)
    ret_move.wait_recv()
    add_up(grad_in, gs, own_ret, back_ret)
    for i, step in enumerate(STEPS):
        spread[i].wait_recv()

    def out_columns(at):
        return pl.ds(pl.multiple_of(at * quarter, quarter), quarter)

    dwo_out[:, out_columns(x_at)] = out_sum[x_at]
    for r in (1, 2, 3):
        dwo_out[:, out_columns(lax.rem(x_at + r, 4))] = out_recv[r - 1]
    for t in (1, 2, 3):
        msgs[t, 6].wait_recv()
        outs[t][...] = total(near[t][0, z_at], last[t][...])
    for made in started:
        made.wait_send()


def on_device(hidden_in, grad_out, w_query, w_key, w_value, w_out, pattern):
    features, half = w_query.shape[1], w_query.shape[2]
    heads = half // HDIM
    vmem = pl.BlockSpec(memory_space=pltpu.VMEM)
    anywhere = pl.BlockSpec(memory_space=pl.ANY)
    ranks = X_SIZE * Z_SIZE * Y_SIZE
    tails = [(half // ranks, features)] + [(features // ranks, half)] * 3
    both, one = (2 * SEQ, features), (SEQ, features)
    scratch = [
        pltpu.VMEM(both, BF16),
        pltpu.VMEM(both, BF16),
        pltpu.VMEM((features, 3 * half), BF16),
        pltpu.VMEM((half, features), BF16),
        pltpu.VMEM((8, 4, features // ranks, 2 * SEQ), BF16),
        pltpu.VMEM((half, 2 * SEQ), BF16),
        pltpu.VMEM((2 * SEQ, 3 * half), BF16),
        pltpu.VMEM((2 * heads, SEQ, SEQ), F32),
        pltpu.VMEM((2 * SEQ, half), BF16),
        pltpu.VMEM((2 * SEQ, 3 * half), BF16),
        pltpu.VMEM((2 * SEQ, 128), F32),
        pltpu.VMEM(one, F32),
    ] + [pltpu.VMEM(one, BF16)] * 6
    quarter = features // 4
    small = (half // ranks, quarter)
    scratch += [
        pltpu.VMEM((3, 8, features // ranks, 2 * SEQ), BF16),
        pltpu.VMEM((3, 2 * SEQ, 3 * half), BF16),
        pltpu.VMEM((3, half, 2 * SEQ), BF16),
        pltpu.VMEM((3, 2 * SEQ, quarter), BF16),
        pltpu.VMEM((4,) + small, F32),
        pltpu.VMEM((3,) + small, F32),
        pltpu.VMEM((X_SIZE, Z_SIZE, Y_SIZE) + small, BF16),
    ] + [pltpu.VMEM((X_SIZE, Z_SIZE) + tails[1], BF16)] * 3
    for lead in ((2,), (2, 2), ()):
        scratch += [pltpu.VMEM(lead + tail, BF16) for tail in [(4,) + small] + tails[1:]]
    scratch += [
        pltpu.SemaphoreType.DMA((6,)),
        pltpu.SemaphoreType.DMA((4,)),
        pltpu.SemaphoreType.DMA((4,)),
        pltpu.SemaphoreType.DMA((4, 10)),
        pltpu.SemaphoreType.DMA((4, 10)),
        pltpu.SemaphoreType.DMA((12, 3)),
        pltpu.SemaphoreType.DMA((12, 3)),
    ]
    outs = pl.pallas_call(
        sublayer_kernel,
        out_shape=(jax.ShapeDtypeStruct(one, BF16),) * 2
        + tuple(jax.ShapeDtypeStruct(tail, F32) for tail in tails[1:] + tails[:1]),
        in_specs=[pl.BlockSpec(memory_space=pltpu.SMEM)] + [anywhere] * 6,
        out_specs=(vmem,) * 6,
        scratch_shapes=scratch,
        compiler_params=pltpu.CompilerParams(
            collective_id=0, has_side_effects=True, vmem_limit_bytes=56 * 1024 * 1024
        ),
        name="sublayer",
    )(pattern, hidden_in, grad_out, w_query[0], w_key[0], w_value[0], w_out[0])
    return (outs[0], outs[1]) + tuple(out[None] for out in outs[2:])


def solution(mesh):
    in_specs = (
        P(("dp", "pipe"), None),
        P(("dp", "pipe"), None),
        P("pipe", None, None),
        P("pipe", None, None),
        P("pipe", None, None),
        P("pipe", None, None),
        P(),
    )
    out_specs = (
        P(("dp", "pipe"), None),
        P(("dp", "pipe"), None),
        P("pipe", "dp", None),
        P("pipe", "dp", None),
        P("pipe", "dp", None),
        P("pipe", "dp", None),
    )
    return jax.shard_map(
        on_device, mesh=mesh, in_specs=in_specs, out_specs=out_specs, check_vma=False
    )
```

```python
import functools
import math

import jax
import jax.numpy as jnp
from jax import lax
from jax.experimental import pallas as pl
from jax.experimental.pallas import tpu as pltpu
from jax.sharding import PartitionSpec as P

HDIM = 64
BLK = 32
SEQ = 128
NORM_EPS = 1e-05
MESH = pl.DeviceIdType.MESH
X_SIZE, Z_SIZE, Y_SIZE = 4, 2, 4
RING_X = (False, True, True, True, False)
STEPS = (1, 3, 2)
BF16 = jnp.bfloat16
F32 = jnp.float32


def dot_nn(a, b):
    return lax.dot_general(a, b, (((1,), (0,)), ((), ())), preferred_element_type=F32)


def dot_nt(a, b):
    return lax.dot_general(a, b, (((1,), (1,)), ((), ())), preferred_element_type=F32)


def dot_tn(a, b):
    return lax.dot_general(a, b, (((0,), (0,)), ((), ())), preferred_element_type=F32)


def total(*terms):
    acc = terms[0].astype(F32)
    for term in terms[1:]:
        acc = acc + term.astype(F32)
    return acc


def sublayer_kernel(*refs):
    pattern, x_in, g_in, wq_in, wk_in, wv_in, wo_in = refs[:7]
    hidden_out, grad_in, dwq_out, dwk_out, dwv_out, dwo_out = refs[7:13]
    (
        xs, gs, w_in, w_out, w_far, norm_t, att_t, qkv, prob, g_att, g_qkv, factor, g_norm,
        own_term, far_term, own_ret, away_ret, back_ret, far_grad_out, far_grad_in, far_att,
        far_own, far_part, far_part_in, term_part,
        norm_y, grad_y, att_x, g_x, out_sum, out_cast, out_own, out_far, out_back,
    ) = refs[13:47]
    parts, far, near, last = (refs[47 + 5 * i : 52 + 5 * i] for i in range(4))
    load_sem, pair_send, pair_recv, ring_send, ring_recv, gather_send, gather_recv = refs[67:74]
    outs = (None, dwv_out, dwq_out, dwk_out)

    features = xs.shape[1]
    half = w_out.shape[0]
    heads = half // HDIM
    inv_sqrt = 1.0 / math.sqrt(HDIM)
    quarter = features // 4

    dp = lax.axis_index("dp")
    pipe = lax.axis_index("pipe")
    slots = lax.axis_size("pipe")
    x_at = dp // (Z_SIZE * Y_SIZE)
    z_at = lax.rem(dp // Y_SIZE, Z_SIZE)
    y_at = lax.rem(dp, Y_SIZE)

    def device(x, z, y):
        return ((x * Z_SIZE + z) * Y_SIZE + y, pipe)

    def x_to(step):
        return device(lax.rem(x_at + step, X_SIZE), z_at, y_at)

    def y_to(step):
        return device(x_at, z_at, lax.rem(y_at + step, Y_SIZE))

    z_mate = device(x_at, 1 - z_at, y_at)
    mirror = (dp, slots - 1 - pipe)

    first, second = pl.ds(0, SEQ), pl.ds(SEQ, SEQ)
    loads = [
        pltpu.make_async_copy(src, dst, load_sem.at[i])
        for i, (src, dst) in enumerate(
            (
                (x_in, xs.at[first]),
                (g_in, gs),
                (wq_in, w_in.at[:, pl.ds(0, half)]),
                (wk_in, w_in.at[:, pl.ds(half, half)]),
                (wv_in, w_in.at[:, pl.ds(2 * half, half)]),
                (wo_in, w_out),
            )
        )
    ]
    for load in loads:
        load.start()

    barrier = pltpu.get_barrier_semaphore()
    for target in (mirror, z_mate) + tuple(to(step) for to in (x_to, y_to) for step in STEPS):
        pl.semaphore_signal(barrier, inc=1, device_id=target, device_id_type=MESH)
    pl.semaphore_wait(barrier, 8)

    started = []

    def send(src, dst, send_sem, recv_sem, target):
        made = pltpu.make_async_remote_copy(
            src_ref=src, dst_ref=dst, send_sem=send_sem, recv_sem=recv_sem, device_id=target, device_id_type=MESH
        )
        made.start()
        started.append(made)
        return made

    def to_mirror(src, dst, slot):
        return send(src, dst, pair_send.at[slot], pair_recv.at[slot], mirror)

    def columns(at):
        return pl.ds(pl.multiple_of(at * quarter, quarter), quarter)

    share = half // (Z_SIZE * Y_SIZE)
    share_rows = pl.ds(pl.multiple_of((z_at * Y_SIZE + y_at) * share, share), share)
    w_move = to_mirror(wo_in.at[share_rows, columns(x_at)], w_far.at[z_at, y_at], 1)
    head_rows = SEQ // 4
    x_moves = [to_mirror(x_in.at[pl.ds(0, head_rows), :], xs.at[pl.ds(SEQ, head_rows), :], 0)]

    gathers = {}

    def gather(kind, src_of, dst_of, to):
        gathers[kind] = [
            send(src_of(step), dst_of(3 - step), gather_send.at[kind, i], gather_recv.at[kind, i], to(step))
            for i, step in enumerate(STEPS)
        ]

    def arrived(*kinds):
        for kind in kinds:
            for move in gathers[kind]:
                move.wait_recv()

    def seq(s):
        return pl.ds(s * SEQ, SEQ)

    def gather_norm(s):
        gather(
            s,
            lambda step: norm_t.at[s, lax.rem(y_at + step, 4)],
            lambda i: norm_y.at[i, s],
            y_to,
        )

    def gather_att(slot):
        rows = pl.ds(slot * half, half)
        gather(2 + slot, lambda step: att_t.at[rows, :], lambda i: att_x.at[i, rows, :], x_to)

    def gather_out_grad():
        def piece(step):
            return gs.at[:, columns(lax.rem(x_at + step, 4))]

        gather(4, piece, lambda i: g_x.at[i], x_to)

    def grad_move(kind, slot, src, dst, step):
        return send(src, dst, gather_send.at[kind, slot], gather_recv.at[kind, slot], y_to(step))

    def gather_grad(s, c):
        kind = 6 + 3 * s + c
        gathers[kind] = [
            grad_move(kind, i, g_qkv.at[c, seq(s)], grad_y.at[3 - step, c, seq(s)], step)
            for i, step in enumerate((1, 3))
        ]

    def relay_grad(s, c):
        kind = 6 + 3 * s + c
        passed = []
        for i, step in enumerate((1, 3)):
            gathers[kind][i].wait_recv()
            rows = pl.ds(s * SEQ + i * (SEQ // 2), SEQ // 2)
            passed.append(grad_move(kind, 2 + i, grad_y.at[3 - step, c, rows], grad_y.at[1, c, rows], step))
        gathers[kind] = passed

    def far_pair():
        w_move.wait_recv()
        src = w_far.at[z_at, y_at]
        gathers[13] = [send(src, src, gather_send.at[13, 0], gather_recv.at[13, 0], z_mate)]

    def far_spread():
        arrived(13)
        src = w_far.at[:, y_at]
        gathers[12] = [
            send(src, src, gather_send.at[12, i], gather_recv.at[12, i], y_to(step)) for i, step in enumerate(STEPS)
        ]

    def far_grad_parts():
        arrived(12, 4)
        far_own[...] = dot_nt(gs[:, columns(x_at)], w_far[...].reshape(half, quarter))
        gathers[14] = []
        for i, step in enumerate(STEPS):
            far_part[step - 1] = dot_nt(g_x[step - 1], w_far[...].reshape(half, quarter)).astype(BF16)
            src, dst = far_part.at[step - 1], far_part_in.at[3 - step]
            gathers[14].append(send(src, dst, gather_send.at[14, i], gather_recv.at[14, i], x_to(step)))

    def far_grad_sum():
        arrived(14)
        far_grad_out[...] = total(far_own[...], far_part_in[0], far_part_in[1], far_part_in[2]).astype(BF16)
        return to_mirror(far_grad_out, far_grad_in, 2)

    def far_term_parts():
        far_term[:, columns(x_at)] = dot_nn(far_att[...], w_far[...].reshape(half, quarter)).astype(BF16)
        gathers[15] = []
        for i, step in enumerate(STEPS):
            theirs = att_x[step - 1, half : 2 * half, :]
            term_part[step - 1] = dot_tn(theirs, w_far[...].reshape(half, quarter)).astype(BF16)
            src, dst = term_part.at[step - 1], far_term.at[:, columns(x_at)]
            gathers[15].append(send(src, dst, gather_send.at[15, i], gather_recv.at[15, i], x_to(step)))

    row = lax.broadcasted_iota(jnp.int32, (SEQ, SEQ), 0)
    col = lax.broadcasted_iota(jnp.int32, (SEQ, SEQ), 1)
    row_block, col_block = row // BLK, col // BLK
    listed = None
    for j in range(pattern.shape[1]):
        entry = jnp.full((SEQ, SEQ), pattern[0, j], jnp.int32)
        for i in range(1, SEQ // BLK):
            entry = jnp.where(row_block == i, pattern[i, j], entry)
        hit = entry == col_block
        listed = hit if listed is None else jnp.logical_or(listed, hit)
    visible = jnp.logical_and(listed, jnp.logical_or(col_block != row_block, col <= row))
    mask = jnp.where(visible, 1.0, 0.0).astype(F32)

    def head(ref, rows, base, h):
        return ref[rows, base + h * HDIM : base + (h + 1) * HDIM]

    def forward_norm(s):
        rows = slice(s * SEQ, (s + 1) * SEQ)
        own_norm = own_ret if s == 0 else away_ret

        def normalise(i, carry):
            at = pl.multiple_of(s * SEQ + i * 16, 16)
            chunk = xs[pl.ds(at, 16), :].astype(F32)
            scale = lax.rsqrt(jnp.mean(chunk * chunk, axis=-1, keepdims=True) + NORM_EPS)
            factor[pl.ds(at, 16), :] = jnp.broadcast_to(scale, (16, 128))
            own_norm[pl.ds(pl.multiple_of(i * 16, 16), 16), :] = (chunk * scale).astype(BF16)
            return carry

        lax.fori_loop(0, SEQ // 16, normalise, 0)
        for c in range(4):
            flipped = own_norm[:, c * quarter : (c + 1) * quarter].T
            tall = norm_t.shape[3]
            for k in range(8):
                norm_t[s, k % 4, 2 * c + k // 4] = flipped[k * tall : (k + 1) * tall, :]

    def forward(s):
        rows = slice(s * SEQ, (s + 1) * SEQ)
        own_norm = own_ret if s == 0 else away_ret
        for c in range(3):
            cols = slice(c * half, (c + 1) * half)
            qkv[rows, cols] = dot_nn(own_norm[...], w_in[:, cols]).astype(BF16)
        wide = min(512, features)
        for h in range(0, heads, 2):
            pair = []
            for hh in (h, h + 1):
                score = dot_nt(head(qkv, rows, 0, hh), head(qkv, rows, half, hh)) * inv_sqrt
                expo = jnp.where(mask > 0.5, jnp.exp(score), 0.0)
                p = expo / jnp.sum(expo, axis=-1, keepdims=True)
                prob[s * heads + hh] = p
                pair.append(dot_nn(p.astype(BF16), head(qkv, rows, 2 * half, hh)).astype(BF16))
            both = jnp.concatenate(pair, axis=1)
            g_att[rows, h * HDIM : (h + 2) * HDIM] = both
        if s == 0:
            att_t[0:half, :] = g_att[rows, :].T
            for c in range(features // wide):
                cols = slice(c * wide, (c + 1) * wide)
                own_term[:, cols] = dot_nn(g_att[rows, :], w_out[:, cols]).astype(BF16)

    def backward_heads(s):
        rows = slice(s * SEQ, (s + 1) * SEQ)
        if s == 0:
            g_att[rows, :] = dot_nt(gs[...], w_out[...]).astype(BF16)
        grad_ref = g_att if s == 0 else far_grad_in
        for h in range(0, heads, 2):
            g_q, g_k, g_v = [], [], []
            for hh in (h, h + 1):
                p = prob[s * heads + hh]
                ga = head(grad_ref, slice(0, SEQ), 0, hh)
                g_prob = dot_nt(ga, head(qkv, rows, 2 * half, hh))
                inner = jnp.sum(p * g_prob, axis=-1, keepdims=True)
                g_score = (p * (g_prob - inner) * inv_sqrt).astype(BF16)
                g_q.append(dot_nn(g_score, head(qkv, rows, half, hh)).astype(BF16))
                g_k.append(dot_tn(g_score, head(qkv, rows, 0, hh)).astype(BF16))
                g_v.append(dot_tn(p.astype(BF16), ga).astype(BF16))
            for c, pieces in enumerate((g_q, g_k, g_v)):
                g_qkv[c, rows, h * HDIM : (h + 2) * HDIM] = jnp.concatenate(pieces, axis=1)

    def backward_input(s):
        rows = slice(s * SEQ, (s + 1) * SEQ)
        wide = min(512, features)
        for c in range(features // wide):
            cols = slice(c * wide, (c + 1) * wide)
            acc = dot_nt(g_qkv[0, rows, :], w_in[cols, 0:half])
            for p in (1, 2):
                acc = acc + dot_nt(g_qkv[p, rows, :], w_in[cols, p * half : (p + 1) * half])
            g_norm[:, cols] = acc
        result = own_ret if s == 0 else away_ret

        def returned(i, carry):
            at = pl.multiple_of(i * 16, 16)
            all_at = pl.multiple_of(s * SEQ + i * 16, 16)
            value = xs[pl.ds(all_at, 16), :].astype(F32)
            grad = g_norm[pl.ds(at, 16), :]
            r = factor[pl.ds(all_at, 16), 0:1]
            mean_term = jnp.mean(value * grad, axis=-1, keepdims=True)
            result[pl.ds(at, 16), :] = (r * grad - value * (r * r * r * mean_term)).astype(BF16)
            return carry

        lax.fori_loop(0, SEQ // 16, returned, 0)

    msgs = {}

    def piece(t, at, z):
        return parts[t].at[at, z] if RING_X[t] else parts[t].at[:, z, at]

    def ring_to(t, step):
        return x_to(step) if RING_X[t] else y_to(step)

    def copy(src, dst, t, slot, target):
        msgs[t, slot] = send(src, dst, ring_send.at[t, slot], ring_recv.at[t, slot], target)

    def ring_start(t):
        at = x_at if RING_X[t] else y_at
        opposite, right, left = (lax.rem(at + step, 4) for step in (2, 1, 3))
        copy(piece(t, opposite, 0), far[t].at[0], t, 0, ring_to(t, 1))
        copy(piece(t, opposite, 1), far[t].at[1], t, 1, ring_to(t, 3))
        copy(piece(t, right, 1), near[t].at[0, 1], t, 2, ring_to(t, 1))
        copy(piece(t, left, 0), near[t].at[1, 0], t, 3, ring_to(t, 3))

    def ring_forward(t):
        at = x_at if RING_X[t] else y_at
        for side, step in ((0, 1), (1, 3)):
            msgs[t, side].wait_recv()
            own = piece(t, lax.rem(at + step, 4), side)[...]
            far[t][side] = total(own, far[t][side]).astype(BF16)
            copy(far[t].at[side], near[t].at[side, side], t, 4 + side, ring_to(t, step))

    def ring_finish(t):
        at = x_at if RING_X[t] else y_at
        for slot in range(2, 6):
            msgs[t, slot].wait_recv()
        for z in range(2):
            own = piece(t, at, z)[...]
            near[t][0, z] = total(own, near[t][0, z], near[t][1, z]).astype(BF16)
        copy(near[t].at[0, 1 - z_at], last[t], t, 6, z_mate)

    def weight_grad(t, c):
        tall = (quarter // 4, SEQ)

        def norm_rows(pair, i):
            return jnp.concatenate([pair(s)[2 * i : 2 * i + 2].reshape(tall) for s in range(2)], axis=1)

        for i in range(X_SIZE):
            acc = dot_nn(norm_rows(lambda s: norm_t.at[s, y_at], i), g_qkv[c])
            for j in range(3):
                acc = acc + dot_nn(norm_rows(lambda s: norm_y.at[j, s], i), grad_y[j, c])
            parts[t][i] = acc.astype(BF16).reshape(parts[t].shape[1:])

    def out_weight_grad(t, slot):
        block = half // X_SIZE
        mine = gs[:, columns(x_at)]
        for i in range(X_SIZE):
            rows = slice(slot * half + i * block, slot * half + (i + 1) * block)
            acc = dot_nn(att_t[rows, :], mine)
            for j in range(3):
                acc = acc + dot_nn(att_x[j, rows, :], g_x[j])
            parts[t][i] = acc.astype(BF16).reshape(parts[t].shape[1:])

    def out_spread(t, pieces, joined):
        msgs[t, 6].wait_recv()
        pieces[...] = total(near[t][0, z_at], last[t][...]).astype(pieces.dtype)
        joined[:, columns(x_at)] = pieces[x_at]
        for i, step in enumerate(STEPS):
            src, dst = pieces.at[lax.rem(x_at + step, 4)], joined.at[:, columns(x_at)]
            msgs[t, 7 + i] = send(src, dst, ring_send.at[t, 7 + i], ring_recv.at[t, 7 + i], x_to(step))

    def out_joined(t):
        for i in range(3):
            msgs[t, 7 + i].wait_recv()

    def add_up(out, base, one, two):
        def body(i, carry):
            at = pl.ds(pl.multiple_of(i * 16, 16), 16)
            out[at, :] = total(base[at, :], one[at, :], two[at, :]).astype(BF16)
            return carry

        lax.fori_loop(0, SEQ // 16, body, 0)

    loads[1].wait()
    gather_out_grad()
    far_pair()
    rest = SEQ - head_rows
    x_moves.append(to_mirror(x_in.at[pl.ds(head_rows, rest), :], xs.at[pl.ds(SEQ + head_rows, rest), :], 6))
    loads[0].wait()
    forward_norm(0)
    far_spread()
    gather_norm(0)
    for load in loads[2:]:
        load.wait()
    forward(0)
    gather_att(0)
    backward_heads(0)
    for c in (2, 0, 1):
        gather_grad(0, c)
    far_grad_parts()
    backward_input(0)
    far_move = far_grad_sum()

    for move in x_moves:
        move.wait_recv()
    forward_norm(1)
    gather_norm(1)
    forward(1)
    att_move = to_mirror(g_att.at[second], far_att, 3)
    for c in (2, 0, 1):
        relay_grad(0, c)
    far_move.wait_recv()
    backward_heads(1)
    for c in (2, 0, 1):
        gather_grad(1, c)
    backward_input(1)
    ret_move = to_mirror(away_ret, back_ret, 4)

    arrived(2)
    out_weight_grad(0, 0)
    ring_start(0)
    att_move.wait_recv()
    att_t[half : 2 * half, :] = far_att[...].T
    gather_att(1)
    relay_grad(1, 2)
    arrived(3)
    out_weight_grad(4, 1)
    relay_grad(1, 0)
    ring_start(4)
    far_term_parts()
    relay_grad(1, 1)
    ring_forward(0)
    arrived(0, 1, 8, 11)
    weight_grad(1, 2)
    ring_start(1)
    arrived(6, 9)
    weight_grad(2, 0)
    ring_start(2)
    ring_forward(4)
    ring_forward(1)
    arrived(7, 10)
    weight_grad(3, 1)
    ring_start(3)
    ring_finish(0)
    ring_finish(4)
    ring_forward(2)
    ring_finish(1)
    ring_forward(3)
    arrived(15)
    add_up(hidden_out, xs, own_term, far_term)
    out_spread(4, out_cast, out_far)
    out_spread(0, out_sum, out_own)
    ring_finish(2)
    out_joined(4)
    out_move = to_mirror(out_far, out_back, 5)
    ring_finish(3)
    ret_move.wait_recv()
    add_up(grad_in, gs, own_ret, back_ret)
    for t in (1, 2, 3):
        msgs[t, 6].wait_recv()
        outs[t][...] = total(near[t][0, z_at], last[t][...])
    out_joined(0)
    out_move.wait_recv()
    dwo_out[...] = total(out_own[...], out_back[...])
    for made in started:
        made.wait_send()


def hand_on_kernel(*refs):
    count = 6
    srcs, dsts, bufs = refs[:count], refs[count : 2 * count], refs[2 * count : 3 * count]
    in_sem, out_sem = refs[3 * count :]
    ins = [pltpu.make_async_copy(srcs[i], bufs[i], in_sem.at[i]) for i in range(count)]
    outs = [pltpu.make_async_copy(bufs[i], dsts[i], out_sem.at[i]) for i in range(count)]
    for move in ins:
        move.start()
    for i in range(count):
        ins[i].wait()
        outs[i].start()
    for move in outs:
        move.wait()


def hand_on(arrays):
    anywhere = pl.BlockSpec(memory_space=pl.ANY)
    return pl.pallas_call(
        hand_on_kernel,
        out_shape=tuple(jax.ShapeDtypeStruct(a.shape, a.dtype) for a in arrays),
        in_specs=[anywhere] * 6,
        out_specs=(anywhere,) * 6,
        scratch_shapes=[pltpu.VMEM(a.shape, a.dtype) for a in arrays]
        + [pltpu.SemaphoreType.DMA((6,)), pltpu.SemaphoreType.DMA((6,))],
        name="hand_on",
    )(*arrays)


def on_device(hidden_in, grad_out, w_query, w_key, w_value, w_out, pattern):
    features, half = w_query.shape[1], w_query.shape[2]
    heads = half // HDIM
    vmem = pl.BlockSpec(memory_space=pltpu.VMEM)
    anywhere = pl.BlockSpec(memory_space=pl.ANY)
    ranks = X_SIZE * Z_SIZE * Y_SIZE
    tails = [(half // ranks, features)] + [(features // ranks, half)] * 3
    both, one = (2 * SEQ, features), (SEQ, features)
    quarter = features // 4
    small = (half // ranks, quarter)
    scratch = [
        pltpu.VMEM(both, BF16),
        pltpu.VMEM(one, BF16),
        pltpu.VMEM((features, 3 * half), BF16),
        pltpu.VMEM((half, features), BF16),
        pltpu.VMEM((Z_SIZE, Y_SIZE, half // 8, quarter), BF16),
        pltpu.VMEM((2, 4, 8, features // ranks, SEQ), BF16),
        pltpu.VMEM((2 * half, SEQ), BF16),
        pltpu.VMEM((2 * SEQ, 3 * half), BF16),
        pltpu.VMEM((2 * heads, SEQ, SEQ), F32),
        pltpu.VMEM((2 * SEQ, half), BF16),
        pltpu.VMEM((3, 2 * SEQ, half), BF16),
        pltpu.VMEM((2 * SEQ, 128), F32),
        pltpu.VMEM(one, F32),
    ] + [pltpu.VMEM(one, BF16)] * 5
    scratch += [pltpu.VMEM((SEQ, half), BF16)] * 3
    scratch += [
        pltpu.VMEM((SEQ, half), F32),
        pltpu.VMEM((3, SEQ, half), BF16),
        pltpu.VMEM((3, SEQ, half), BF16),
        pltpu.VMEM((3, SEQ, quarter), BF16),
    ]
    scratch += [
        pltpu.VMEM((3, 2, 8, features // ranks, SEQ), BF16),
        pltpu.VMEM((3, 3, 2 * SEQ, half), BF16),
        pltpu.VMEM((3, 2 * half, SEQ), BF16),
        pltpu.VMEM((3, SEQ, quarter), BF16),
        pltpu.VMEM((4,) + small, F32),
        pltpu.VMEM((4,) + small, BF16),
        pltpu.VMEM(tails[0], F32),
        pltpu.VMEM(tails[0], BF16),
        pltpu.VMEM(tails[0], BF16),
    ]
    lead = (X_SIZE, Z_SIZE)
    scratch += (
        [pltpu.VMEM(lead + (Y_SIZE,) + small, BF16)]
        + [pltpu.VMEM(lead + tails[1], BF16)] * 3
        + [pltpu.VMEM(lead + (Y_SIZE,) + small, BF16)]
    )
    for lead in ((2,), (2, 2), ()):
        scratch += [pltpu.VMEM(lead + tail, BF16) for tail in [(4,) + small] + tails[1:] + [(4,) + small]]
    scratch += [
        pltpu.SemaphoreType.DMA((6,)),
        pltpu.SemaphoreType.DMA((7,)),
        pltpu.SemaphoreType.DMA((7,)),
        pltpu.SemaphoreType.DMA((5, 10)),
        pltpu.SemaphoreType.DMA((5, 10)),
        pltpu.SemaphoreType.DMA((16, 4)),
        pltpu.SemaphoreType.DMA((16, 4)),
    ]
    outs = pl.pallas_call(
        sublayer_kernel,
        out_shape=(jax.ShapeDtypeStruct(one, BF16),) * 2
        + tuple(jax.ShapeDtypeStruct(tail, F32) for tail in tails[1:] + tails[:1]),
        in_specs=[pl.BlockSpec(memory_space=pltpu.SMEM)] + [anywhere] * 6,
        out_specs=(vmem,) * 6,
        scratch_shapes=scratch,
        compiler_params=pltpu.CompilerParams(
            collective_id=0, has_side_effects=True, vmem_limit_bytes=56 * 1024 * 1024
        ),
        name="sublayer",
    )(pattern, hidden_in, grad_out, w_query[0], w_key[0], w_value[0], w_out[0])
    outs = hand_on(outs)
    return (outs[0], outs[1]) + tuple(out[None] for out in outs[2:])


def solution(mesh):
    in_specs = (
        P(("dp", "pipe"), None),
        P(("dp", "pipe"), None),
        P("pipe", None, None),
        P("pipe", None, None),
        P("pipe", None, None),
        P("pipe", None, None),
        P(),
    )
    out_specs = (
        P(("dp", "pipe"), None),
        P(("dp", "pipe"), None),
        P("pipe", "dp", None),
        P("pipe", "dp", None),
        P("pipe", "dp", None),
        P("pipe", "dp", None),
    )
    return jax.shard_map(
        on_device, mesh=mesh, in_specs=in_specs, out_specs=out_specs, check_vma=False
    )
```

```python
import functools
import math

import jax
import jax.numpy as jnp
from jax import lax
from jax.experimental import pallas as pl
from jax.experimental.pallas import tpu as pltpu
from jax.sharding import PartitionSpec as P

HDIM = 64
BLK = 32
SEQ = 128
NORM_EPS = 1e-05
MESH = pl.DeviceIdType.MESH
X_SIZE, Z_SIZE, Y_SIZE = 4, 2, 4
RING_X = (False, True, True, True, False)
STEPS = (1, 3, 2)
BF16 = jnp.bfloat16
F32 = jnp.float32


def dot_nn(a, b):
    return lax.dot_general(a, b, (((1,), (0,)), ((), ())), preferred_element_type=F32)


def dot_nt(a, b):
    return lax.dot_general(a, b, (((1,), (1,)), ((), ())), preferred_element_type=F32)


def dot_tn(a, b):
    return lax.dot_general(a, b, (((0,), (0,)), ((), ())), preferred_element_type=F32)


def total(*terms):
    acc = terms[0].astype(F32)
    for term in terms[1:]:
        acc = acc + term.astype(F32)
    return acc


def sublayer_kernel(*refs):
    pattern, x_in, g_in, wq_in, wk_in, wv_in, wo_in = refs[:7]
    hidden_out, grad_in, dwq_out, dwk_out, dwv_out, dwo_out = refs[7:13]
    (
        xs, gs, w_in, w_out, w_far, norm_t, att_t, qkv, prob, g_att, g_qkv, factor, g_norm,
        own_term, far_term, own_ret, away_ret, back_ret, far_grad_out, far_grad_in, far_att,
        far_own, far_part, far_part_in, term_part,
        norm_y, grad_y, att_x, g_x, out_sum, out_cast, out_own, out_far, out_back,
    ) = refs[13:47]
    parts, far, near, last = (refs[47 + 5 * i : 52 + 5 * i] for i in range(4))
    load_sem, pair_send, pair_recv, ring_send, ring_recv, gather_send, gather_recv = refs[67:74]
    outs = (None, dwv_out, dwq_out, dwk_out)

    features = xs.shape[1]
    half = w_out.shape[0]
    heads = half // HDIM
    inv_sqrt = 1.0 / math.sqrt(HDIM)
    quarter = features // 4

    dp = lax.axis_index("dp")
    pipe = lax.axis_index("pipe")
    slots = lax.axis_size("pipe")
    x_at = dp // (Z_SIZE * Y_SIZE)
    z_at = lax.rem(dp // Y_SIZE, Z_SIZE)
    y_at = lax.rem(dp, Y_SIZE)

    def device(x, z, y):
        return ((x * Z_SIZE + z) * Y_SIZE + y, pipe)

    def x_to(step):
        return device(lax.rem(x_at + step, X_SIZE), z_at, y_at)

    def y_to(step):
        return device(x_at, z_at, lax.rem(y_at + step, Y_SIZE))

    z_mate = device(x_at, 1 - z_at, y_at)
    mirror = (dp, slots - 1 - pipe)

    first, second = pl.ds(0, SEQ), pl.ds(SEQ, SEQ)
    loads = [
        pltpu.make_async_copy(src, dst, load_sem.at[i])
        for i, (src, dst) in enumerate(
            (
                (x_in, xs.at[first]),
                (g_in, gs),
                (wq_in, w_in.at[:, pl.ds(0, half)]),
                (wk_in, w_in.at[:, pl.ds(half, half)]),
                (wv_in, w_in.at[:, pl.ds(2 * half, half)]),
                (wo_in, w_out),
            )
        )
    ]
    for load in loads:
        load.start()

    barrier = pltpu.get_barrier_semaphore()
    for target in (mirror, z_mate) + tuple(to(step) for to in (x_to, y_to) for step in STEPS):
        pl.semaphore_signal(barrier, inc=1, device_id=target, device_id_type=MESH)
    pl.semaphore_wait(barrier, 8)

    started = []

    def send(src, dst, send_sem, recv_sem, target):
        made = pltpu.make_async_remote_copy(
            src_ref=src, dst_ref=dst, send_sem=send_sem, recv_sem=recv_sem, device_id=target, device_id_type=MESH
        )
        made.start()
        started.append(made)
        return made

    def to_mirror(src, dst, slot):
        return send(src, dst, pair_send.at[slot], pair_recv.at[slot], mirror)

    def columns(at):
        return pl.ds(pl.multiple_of(at * quarter, quarter), quarter)

    share = half // (Z_SIZE * Y_SIZE)
    share_rows = pl.ds(pl.multiple_of((z_at * Y_SIZE + y_at) * share, share), share)
    w_move = to_mirror(wo_in.at[share_rows, columns(x_at)], w_far.at[z_at, y_at], 1)
    head_rows = SEQ // 4
    x_moves = [to_mirror(x_in.at[pl.ds(0, head_rows), :], xs.at[pl.ds(SEQ, head_rows), :], 0)]

    gathers = {}

    def gather(kind, src_of, dst_of, to):
        gathers[kind] = [
            send(src_of(step), dst_of(3 - step), gather_send.at[kind, i], gather_recv.at[kind, i], to(step))
            for i, step in enumerate(STEPS)
        ]

    def arrived(*kinds):
        for kind in kinds:
            for move in gathers[kind]:
                move.wait_recv()

    def seq(s):
        return pl.ds(s * SEQ, SEQ)

    def gather_norm(s):
        gather(
            s,
            lambda step: norm_t.at[s, lax.rem(y_at + step, 4)],
            lambda i: norm_y.at[i, s],
            y_to,
        )

    def gather_att(slot):
        rows = pl.ds(slot * half, half)
        gather(2 + slot, lambda step: att_t.at[rows, :], lambda i: att_x.at[i, rows, :], x_to)

    def gather_out_grad():
        def piece(step):
            return gs.at[:, columns(lax.rem(x_at + step, 4))]

        gather(4, piece, lambda i: g_x.at[i], x_to)

    def grad_move(kind, slot, src, dst, step):
        return send(src, dst, gather_send.at[kind, slot], gather_recv.at[kind, slot], y_to(step))

    def gather_grad(s, c):
        kind = 6 + 3 * s + c
        gathers[kind] = [
            grad_move(kind, i, g_qkv.at[c, seq(s)], grad_y.at[3 - step, c, seq(s)], step)
            for i, step in enumerate((1, 3))
        ]

    def relay_grad(s, c):
        kind = 6 + 3 * s + c
        passed = []
        for i, step in enumerate((1, 3)):
            gathers[kind][i].wait_recv()
            rows = pl.ds(s * SEQ + i * (SEQ // 2), SEQ // 2)
            passed.append(grad_move(kind, 2 + i, grad_y.at[3 - step, c, rows], grad_y.at[1, c, rows], step))
        gathers[kind] = passed

    def far_pair():
        w_move.wait_recv()
        src = w_far.at[z_at, y_at]
        gathers[13] = [send(src, src, gather_send.at[13, 0], gather_recv.at[13, 0], z_mate)]

    def far_spread():
        arrived(13)
        src = w_far.at[:, y_at]
        gathers[12] = [
            send(src, src, gather_send.at[12, i], gather_recv.at[12, i], y_to(step)) for i, step in enumerate(STEPS)
        ]

    def far_grad_parts():
        arrived(12, 4)
        far_own[...] = dot_nt(gs[:, columns(x_at)], w_far[...].reshape(half, quarter))
        gathers[14] = []
        for i, step in enumerate(STEPS):
            far_part[step - 1] = dot_nt(g_x[step - 1], w_far[...].reshape(half, quarter)).astype(BF16)
            src, dst = far_part.at[step - 1], far_part_in.at[3 - step]
            gathers[14].append(send(src, dst, gather_send.at[14, i], gather_recv.at[14, i], x_to(step)))

    def far_grad_sum():
        arrived(14)
        far_grad_out[...] = total(far_own[...], far_part_in[0], far_part_in[1], far_part_in[2]).astype(BF16)
        return to_mirror(far_grad_out, far_grad_in, 2)

    def far_term_parts():
        far_term[:, columns(x_at)] = dot_nn(far_att[...], w_far[...].reshape(half, quarter)).astype(BF16)
        gathers[15] = []
        for i, step in enumerate(STEPS):
            theirs = att_x[step - 1, half : 2 * half, :]
            term_part[step - 1] = dot_tn(theirs, w_far[...].reshape(half, quarter)).astype(BF16)
            src, dst = term_part.at[step - 1], far_term.at[:, columns(x_at)]
            gathers[15].append(send(src, dst, gather_send.at[15, i], gather_recv.at[15, i], x_to(step)))

    row = lax.broadcasted_iota(jnp.int32, (SEQ, SEQ), 0)
    col = lax.broadcasted_iota(jnp.int32, (SEQ, SEQ), 1)
    row_block, col_block = row // BLK, col // BLK
    listed = None
    for j in range(pattern.shape[1]):
        entry = jnp.full((SEQ, SEQ), pattern[0, j], jnp.int32)
        for i in range(1, SEQ // BLK):
            entry = jnp.where(row_block == i, pattern[i, j], entry)
        hit = entry == col_block
        listed = hit if listed is None else jnp.logical_or(listed, hit)
    visible = jnp.logical_and(listed, jnp.logical_or(col_block != row_block, col <= row))
    mask = jnp.where(visible, 1.0, 0.0).astype(F32)

    def head(ref, rows, base, h):
        return ref[rows, base + h * HDIM : base + (h + 1) * HDIM]

    def forward_norm(s):
        rows = slice(s * SEQ, (s + 1) * SEQ)
        own_norm = own_ret if s == 0 else away_ret

        def normalise(i, carry):
            at = pl.multiple_of(s * SEQ + i * 16, 16)
            chunk = xs[pl.ds(at, 16), :].astype(F32)
            scale = lax.rsqrt(jnp.mean(chunk * chunk, axis=-1, keepdims=True) + NORM_EPS)
            factor[pl.ds(at, 16), :] = jnp.broadcast_to(scale, (16, 128))
            own_norm[pl.ds(pl.multiple_of(i * 16, 16), 16), :] = (chunk * scale).astype(BF16)
            return carry

        lax.fori_loop(0, SEQ // 16, normalise, 0)
        for c in range(4):
            flipped = own_norm[:, c * quarter : (c + 1) * quarter].T
            tall = norm_t.shape[3]
            for k in range(8):
                norm_t[s, k % 4, 2 * c + k // 4] = flipped[k * tall : (k + 1) * tall, :]

    def forward(s):
        rows = slice(s * SEQ, (s + 1) * SEQ)
        own_norm = own_ret if s == 0 else away_ret
        for c in range(3):
            cols = slice(c * half, (c + 1) * half)
            qkv[rows, cols] = dot_nn(own_norm[...], w_in[:, cols]).astype(BF16)
        wide = min(512, features)
        for h in range(0, heads, 2):
            pair = []
            for hh in (h, h + 1):
                score = dot_nt(head(qkv, rows, 0, hh), head(qkv, rows, half, hh)) * inv_sqrt
                expo = jnp.where(mask > 0.5, jnp.exp(score), 0.0)
                p = expo / jnp.sum(expo, axis=-1, keepdims=True)
                prob[s * heads + hh] = p
                pair.append(dot_nn(p.astype(BF16), head(qkv, rows, 2 * half, hh)).astype(BF16))
            both = jnp.concatenate(pair, axis=1)
            g_att[rows, h * HDIM : (h + 2) * HDIM] = both
        if s == 0:
            att_t[0:half, :] = g_att[rows, :].T
            for c in range(features // wide):
                cols = slice(c * wide, (c + 1) * wide)
                own_term[:, cols] = dot_nn(g_att[rows, :], w_out[:, cols]).astype(BF16)

    def backward_heads(s):
        rows = slice(s * SEQ, (s + 1) * SEQ)
        if s == 0:
            g_att[rows, :] = dot_nt(gs[...], w_out[...]).astype(BF16)
        grad_ref = g_att if s == 0 else far_grad_in
        for h in range(0, heads, 2):
            g_q, g_k, g_v = [], [], []
            for hh in (h, h + 1):
                p = prob[s * heads + hh]
                ga = head(grad_ref, slice(0, SEQ), 0, hh)
                g_prob = dot_nt(ga, head(qkv, rows, 2 * half, hh))
                inner = jnp.sum(p * g_prob, axis=-1, keepdims=True)
                g_score = (p * (g_prob - inner) * inv_sqrt).astype(BF16)
                g_q.append(dot_nn(g_score, head(qkv, rows, half, hh)).astype(BF16))
                g_k.append(dot_tn(g_score, head(qkv, rows, 0, hh)).astype(BF16))
                g_v.append(dot_tn(p.astype(BF16), ga).astype(BF16))
            for c, pieces in enumerate((g_q, g_k, g_v)):
                g_qkv[c, rows, h * HDIM : (h + 2) * HDIM] = jnp.concatenate(pieces, axis=1)

    def backward_input(s):
        rows = slice(s * SEQ, (s + 1) * SEQ)
        wide = min(512, features)
        for c in range(features // wide):
            cols = slice(c * wide, (c + 1) * wide)
            acc = dot_nt(g_qkv[0, rows, :], w_in[cols, 0:half])
            for p in (1, 2):
                acc = acc + dot_nt(g_qkv[p, rows, :], w_in[cols, p * half : (p + 1) * half])
            g_norm[:, cols] = acc
        result = own_ret if s == 0 else away_ret

        def returned(i, carry):
            at = pl.multiple_of(i * 16, 16)
            all_at = pl.multiple_of(s * SEQ + i * 16, 16)
            value = xs[pl.ds(all_at, 16), :].astype(F32)
            grad = g_norm[pl.ds(at, 16), :]
            r = factor[pl.ds(all_at, 16), 0:1]
            mean_term = jnp.mean(value * grad, axis=-1, keepdims=True)
            result[pl.ds(at, 16), :] = (r * grad - value * (r * r * r * mean_term)).astype(BF16)
            return carry

        lax.fori_loop(0, SEQ // 16, returned, 0)

    msgs = {}

    def piece(t, at, z):
        return parts[t].at[at, z] if RING_X[t] else parts[t].at[:, z, at]

    def ring_to(t, step):
        return x_to(step) if RING_X[t] else y_to(step)

    def copy(src, dst, t, slot, target):
        msgs[t, slot] = send(src, dst, ring_send.at[t, slot], ring_recv.at[t, slot], target)

    def ring_start(t):
        at = x_at if RING_X[t] else y_at
        opposite, right, left = (lax.rem(at + step, 4) for step in (2, 1, 3))
        copy(piece(t, opposite, 0), far[t].at[0], t, 0, ring_to(t, 1))
        copy(piece(t, opposite, 1), far[t].at[1], t, 1, ring_to(t, 3))
        copy(piece(t, right, 1), near[t].at[0, 1], t, 2, ring_to(t, 1))
        copy(piece(t, left, 0), near[t].at[1, 0], t, 3, ring_to(t, 3))

    def ring_forward(t):
        at = x_at if RING_X[t] else y_at
        for side, step in ((0, 1), (1, 3)):
            msgs[t, side].wait_recv()
            own = piece(t, lax.rem(at + step, 4), side)[...]
            far[t][side] = total(own, far[t][side]).astype(BF16)
            copy(far[t].at[side], near[t].at[side, side], t, 4 + side, ring_to(t, step))

    def ring_finish(t):
        at = x_at if RING_X[t] else y_at
        for slot in range(2, 6):
            msgs[t, slot].wait_recv()
        for z in range(2):
            own = piece(t, at, z)[...]
            near[t][0, z] = total(own, near[t][0, z], near[t][1, z]).astype(BF16)
        copy(near[t].at[0, 1 - z_at], last[t], t, 6, z_mate)

    def weight_grad(t, c):
        tall = (quarter // 4, SEQ)

        def norm_rows(pair, i):
            return jnp.concatenate([pair(s)[2 * i : 2 * i + 2].reshape(tall) for s in range(2)], axis=1)

        for i in range(X_SIZE):
            acc = dot_nn(norm_rows(lambda s: norm_t.at[s, y_at], i), g_qkv[c])
            for j in range(3):
                acc = acc + dot_nn(norm_rows(lambda s: norm_y.at[j, s], i), grad_y[j, c])
            parts[t][i] = acc.astype(BF16).reshape(parts[t].shape[1:])

    def out_weight_grad(t, slot):
        block = half // X_SIZE
        mine = gs[:, columns(x_at)]
        for i in range(X_SIZE):
            rows = slice(slot * half + i * block, slot * half + (i + 1) * block)
            acc = dot_nn(att_t[rows, :], mine)
            for j in range(3):
                acc = acc + dot_nn(att_x[j, rows, :], g_x[j])
            parts[t][i] = acc.astype(BF16).reshape(parts[t].shape[1:])

    def out_spread(t, pieces, joined):
        msgs[t, 6].wait_recv()
        pieces[...] = total(near[t][0, z_at], last[t][...]).astype(pieces.dtype)
        joined[:, columns(x_at)] = pieces[x_at]
        for i, step in enumerate(STEPS):
            src, dst = pieces.at[lax.rem(x_at + step, 4)], joined.at[:, columns(x_at)]
            msgs[t, 7 + i] = send(src, dst, ring_send.at[t, 7 + i], ring_recv.at[t, 7 + i], x_to(step))

    def out_joined(t):
        for i in range(3):
            msgs[t, 7 + i].wait_recv()

    def add_up(out, base, one, two):
        def body(i, carry):
            at = pl.ds(pl.multiple_of(i * 16, 16), 16)
            out[at, :] = total(base[at, :], one[at, :], two[at, :]).astype(BF16)
            return carry

        lax.fori_loop(0, SEQ // 16, body, 0)

    loads[1].wait()
    gather_out_grad()
    far_pair()
    rest = SEQ - head_rows
    x_moves.append(to_mirror(x_in.at[pl.ds(head_rows, rest), :], xs.at[pl.ds(SEQ + head_rows, rest), :], 6))
    loads[0].wait()
    forward_norm(0)
    far_spread()
    gather_norm(0)
    for load in loads[2:]:
        load.wait()
    forward(0)
    gather_att(0)
    backward_heads(0)
    for c in (2, 0, 1):
        gather_grad(0, c)
    far_grad_parts()
    backward_input(0)
    far_move = far_grad_sum()

    for move in x_moves:
        move.wait_recv()
    forward_norm(1)
    gather_norm(1)
    forward(1)
    att_move = to_mirror(g_att.at[second], far_att, 3)
    for c in (2, 0, 1):
        relay_grad(0, c)
    far_move.wait_recv()
    backward_heads(1)
    for c in (2, 0, 1):
        gather_grad(1, c)
    backward_input(1)
    ret_move = to_mirror(away_ret, back_ret, 4)

    att_move.wait_recv()
    att_t[half : 2 * half, :] = far_att[...].T
    gather_att(1)
    arrived(2)
    out_weight_grad(0, 0)
    relay_grad(1, 2)
    relay_grad(1, 0)
    arrived(3)
    out_weight_grad(4, 1)
    relay_grad(1, 1)
    ring_start(0)
    ring_start(4)
    arrived(0, 1, 8, 11)
    weight_grad(1, 2)
    ring_start(1)
    arrived(6, 9)
    weight_grad(2, 0)
    ring_start(2)
    ring_forward(1)
    arrived(7, 10)
    weight_grad(3, 1)
    ring_start(3)
    far_term_parts()
    ring_forward(0)
    ring_forward(4)
    ring_forward(2)
    ring_finish(0)
    ring_finish(4)
    ring_forward(3)
    ring_finish(1)
    out_spread(4, out_cast, out_far)
    out_spread(0, out_sum, out_own)
    ring_finish(2)
    out_joined(4)
    out_move = to_mirror(out_far, out_back, 5)
    ring_finish(3)
    arrived(15)
    add_up(hidden_out, xs, own_term, far_term)
    ret_move.wait_recv()
    add_up(grad_in, gs, own_ret, back_ret)
    for t in (1, 2, 3):
        msgs[t, 6].wait_recv()
        outs[t][...] = total(near[t][0, z_at], last[t][...])
    out_joined(0)
    out_move.wait_recv()
    dwo_out[...] = total(out_own[...], out_back[...])
    for made in started:
        made.wait_send()


def hand_on_kernel(*refs):
    count = 6
    srcs, dsts, bufs = refs[:count], refs[count : 2 * count], refs[2 * count : 3 * count]
    in_sem, out_sem = refs[3 * count :]
    ins = [pltpu.make_async_copy(srcs[i], bufs[i], in_sem.at[i]) for i in range(count)]
    outs = [pltpu.make_async_copy(bufs[i], dsts[i], out_sem.at[i]) for i in range(count)]
    for move in ins:
        move.start()
    for i in range(count):
        ins[i].wait()
        outs[i].start()
    for move in outs:
        move.wait()


def hand_on(arrays):
    anywhere = pl.BlockSpec(memory_space=pl.ANY)
    return pl.pallas_call(
        hand_on_kernel,
        out_shape=tuple(jax.ShapeDtypeStruct(a.shape, a.dtype) for a in arrays),
        in_specs=[anywhere] * 6,
        out_specs=(anywhere,) * 6,
        scratch_shapes=[pltpu.VMEM(a.shape, a.dtype) for a in arrays]
        + [pltpu.SemaphoreType.DMA((6,)), pltpu.SemaphoreType.DMA((6,))],
        name="hand_on",
    )(*arrays)


def on_device(hidden_in, grad_out, w_query, w_key, w_value, w_out, pattern):
    features, half = w_query.shape[1], w_query.shape[2]
    heads = half // HDIM
    vmem = pl.BlockSpec(memory_space=pltpu.VMEM)
    anywhere = pl.BlockSpec(memory_space=pl.ANY)
    ranks = X_SIZE * Z_SIZE * Y_SIZE
    tails = [(half // ranks, features)] + [(features // ranks, half)] * 3
    both, one = (2 * SEQ, features), (SEQ, features)
    quarter = features // 4
    small = (half // ranks, quarter)
    scratch = [
        pltpu.VMEM(both, BF16),
        pltpu.VMEM(one, BF16),
        pltpu.VMEM((features, 3 * half), BF16),
        pltpu.VMEM((half, features), BF16),
        pltpu.VMEM((Z_SIZE, Y_SIZE, half // 8, quarter), BF16),
        pltpu.VMEM((2, 4, 8, features // ranks, SEQ), BF16),
        pltpu.VMEM((2 * half, SEQ), BF16),
        pltpu.VMEM((2 * SEQ, 3 * half), BF16),
        pltpu.VMEM((2 * heads, SEQ, SEQ), F32),
        pltpu.VMEM((2 * SEQ, half), BF16),
        pltpu.VMEM((3, 2 * SEQ, half), BF16),
        pltpu.VMEM((2 * SEQ, 128), F32),
        pltpu.VMEM(one, F32),
    ] + [pltpu.VMEM(one, BF16)] * 5
    scratch += [pltpu.VMEM((SEQ, half), BF16)] * 3
    scratch += [
        pltpu.VMEM((SEQ, half), F32),
        pltpu.VMEM((3, SEQ, half), BF16),
        pltpu.VMEM((3, SEQ, half), BF16),
        pltpu.VMEM((3, SEQ, quarter), BF16),
    ]
    scratch += [
        pltpu.VMEM((3, 2, 8, features // ranks, SEQ), BF16),
        pltpu.VMEM((3, 3, 2 * SEQ, half), BF16),
        pltpu.VMEM((3, 2 * half, SEQ), BF16),
        pltpu.VMEM((3, SEQ, quarter), BF16),
        pltpu.VMEM((4,) + small, F32),
        pltpu.VMEM((4,) + small, BF16),
        pltpu.VMEM(tails[0], F32),
        pltpu.VMEM(tails[0], BF16),
        pltpu.VMEM(tails[0], BF16),
    ]
    lead = (X_SIZE, Z_SIZE)
    scratch += (
        [pltpu.VMEM(lead + (Y_SIZE,) + small, BF16)]
        + [pltpu.VMEM(lead + tails[1], BF16)] * 3
        + [pltpu.VMEM(lead + (Y_SIZE,) + small, BF16)]
    )
    for lead in ((2,), (2, 2), ()):
        scratch += [pltpu.VMEM(lead + tail, BF16) for tail in [(4,) + small] + tails[1:] + [(4,) + small]]
    scratch += [
        pltpu.SemaphoreType.DMA((6,)),
        pltpu.SemaphoreType.DMA((7,)),
        pltpu.SemaphoreType.DMA((7,)),
        pltpu.SemaphoreType.DMA((5, 10)),
        pltpu.SemaphoreType.DMA((5, 10)),
        pltpu.SemaphoreType.DMA((16, 4)),
        pltpu.SemaphoreType.DMA((16, 4)),
    ]
    outs = pl.pallas_call(
        sublayer_kernel,
        out_shape=(jax.ShapeDtypeStruct(one, BF16),) * 2
        + tuple(jax.ShapeDtypeStruct(tail, F32) for tail in tails[1:] + tails[:1]),
        in_specs=[pl.BlockSpec(memory_space=pltpu.SMEM)] + [anywhere] * 6,
        out_specs=(vmem,) * 6,
        scratch_shapes=scratch,
        compiler_params=pltpu.CompilerParams(
            collective_id=0, has_side_effects=True, vmem_limit_bytes=56 * 1024 * 1024
        ),
        name="sublayer",
    )(pattern, hidden_in, grad_out, w_query[0], w_key[0], w_value[0], w_out[0])
    outs = hand_on(outs)
    return (outs[0], outs[1]) + tuple(out[None] for out in outs[2:])


def solution(mesh):
    in_specs = (
        P(("dp", "pipe"), None),
        P(("dp", "pipe"), None),
        P("pipe", None, None),
        P("pipe", None, None),
        P("pipe", None, None),
        P("pipe", None, None),
        P(),
    )
    out_specs = (
        P(("dp", "pipe"), None),
        P(("dp", "pipe"), None),
        P("pipe", "dp", None),
        P("pipe", "dp", None),
        P("pipe", "dp", None),
        P("pipe", "dp", None),
    )
    return jax.shard_map(
        on_device, mesh=mesh, in_specs=in_specs, out_specs=out_specs, check_vma=False
    )
```
